128 devices in a mesh: az: 16 (over z_lo, x, core), rg: 8 (over z_hi, y).
Axes of the slice: x: 4, y: 4, z: 4 (z_hi: 2, z_lo: 2; z = z_hi * 2 + z_lo), core: 2. Of those that a mesh axis runs over, the one named last changes fastest.
Arguments:
- raw: bfloat16 [2, 8192, 16384], P(None, 'az', 'rg'), may hold values from -6 to 6
- chirp: bfloat16 [2, 256], replicated, may hold values from -0.25 to 0.25
- az_ref: bfloat16 [2, 64, 512], replicated, may hold values from -0.1875 to 0.1875
- set_index: int32 [16384], P('rg'), may hold values from 0 to 63, as said below
Outputs:
- focused: bfloat16 [2, 8192, 16384], P(None, 'az', 'rg')
The draws below stay inside these ranges and needn't reach their ends.
Inputs may be any that keep to these rules, and one draw needn't show every extreme that they name: `set_index`: range columns come in aligned runs of 128 that share one set index.
All inputs are finite; a program needn't handle non-finite values.
Results may differ from the reference program's by a relative error of at most 0.0049.
Values may be sent and summed in bfloat16 or wider, within the bound.
No kernel may reach another device: no remote copies, remote signals or barrier semaphores. Data moves between devices by JAX's collectives and lax.ppermute only.
A program may use at most 64 MiB of HBM per device.

```python
import jax
import jax.numpy as jnp
from jax import lax

KR = 256
KA = 512
SETS = 64
AZ_TOTAL = 8192
RG_TOTAL = 16384
SET_RUN = 128


def draw_set_index(key, part):
    group_count = RG_TOTAL // SET_RUN
    baseline = jnp.arange(group_count, dtype=jnp.int32) * SETS // group_count
    jitter = jax.random.randint(key, (group_count,), -1, 2).astype(jnp.int32)
    values = jnp.clip(baseline + jitter, 0, SETS - 1)
    values = values.at[0].set(0).at[group_count - 1].set(SETS - 1)
    return jnp.repeat(values, SET_RUN).astype(jnp.int32)


def steps_of(own_key, extent, pieces, smallest, top_value):
    def one(axis_at, shards_of):
        steps = jax.random.uniform(jax.random.fold_in(jax.random.fold_in(own_key, 6), axis_at), (shards_of,), jnp.float32, smallest / len(pieces), top_value / len(pieces))
        return jnp.repeat(jnp.exp(steps), extent[axis_at] // shards_of).reshape((-1,) + (1,) * (len(extent) - axis_at - 1))

    factor_of = one(*pieces[0])
    for cut in pieces[1:]:
        factor_of = factor_of * one(*cut)
    return factor_of


def centred(stream_key, dims, spread, limit, pieces=(), kind=jnp.bfloat16):
    array = spread * jax.random.normal(stream_key, dims, jnp.float32)
    if pieces:
        array = array * steps_of(stream_key, dims, pieces, -0.22, 0.18)
    return jnp.clip(array, -limit, limit).astype(kind)


def setup_inputs(seed: int = 0) -> dict:
    splits = jax.random.split(jax.random.key(seed), 5)
    raw = centred(splits[0], (2, AZ_TOTAL, RG_TOTAL), 1.0, 6.0, ((1, 16), (2, 8)))
    chirp = centred(splits[1], (2, KR), (2 * KR) ** -0.5, 0.25)
    az_ref = centred(splits[2], (2, SETS, KA), (2 * KA) ** -0.5, 0.1875)
    set_index = draw_set_index(jax.random.fold_in(splits[4], 71), 0)
    return {"raw": raw, "chirp": chirp, "az_ref": az_ref, "set_index": set_index}


def reference(raw, chirp, az_ref, set_index):
    lines = raw.shape[1]
    columns = raw.shape[2]
    range_taps = chirp.shape[1]
    azimuth_taps = az_ref.shape[2]
    range_len = columns + range_taps
    chirp_c = lax.complex(chirp[0].astype(jnp.float32), chirp[1].astype(jnp.float32))
    chirp_f = jnp.conj(jnp.fft.fft(chirp_c, range_len))
    block_lines = min(512, lines)

    def range_block(segment):
        signal = lax.complex(segment[0].astype(jnp.float32), segment[1].astype(jnp.float32))
        spectrum = jnp.fft.fft(signal, range_len, axis=1) * chirp_f[None, :]
        result = jnp.fft.ifft(spectrum, axis=1)[:, :columns]
        return jnp.stack([jnp.real(result), jnp.imag(result)]).astype(jnp.bfloat16)

    raw_blocks = raw.reshape(2, lines // block_lines, block_lines, columns).transpose(1, 0, 2, 3)
    compressed = lax.map(range_block, raw_blocks).transpose(1, 0, 2, 3).reshape(2, lines, columns)

    azimuth_len = lines + azimuth_taps
    ref_c = lax.complex(az_ref[0].astype(jnp.float32), az_ref[1].astype(jnp.float32))
    ref_f = jnp.conj(jnp.fft.fft(ref_c, azimuth_len, axis=1))
    block_columns = min(512, columns)
    count = columns // block_columns

    def azimuth_block(inputs):
        segment, chosen = inputs
        signal = lax.complex(segment[0].astype(jnp.float32), segment[1].astype(jnp.float32))
        spectrum = jnp.fft.fft(signal, azimuth_len, axis=0) * jnp.take(ref_f, chosen, axis=0).T
        result = jnp.fft.ifft(spectrum, axis=0)[:lines]
        return jnp.stack([jnp.real(result), jnp.imag(result)]).astype(jnp.bfloat16)

    column_blocks = compressed.reshape(2, lines, count, block_columns).transpose(2, 0, 1, 3)
    set_blocks = set_index.reshape(count, block_columns).astype(jnp.int32)
    focused = lax.map(azimuth_block, (column_blocks, set_blocks))
    return focused.transpose(1, 2, 0, 3).reshape(2, lines, columns)
```

```python
import functools

import jax
import jax.numpy as jnp
from jax import lax
from jax.experimental import pallas as pl
from jax.experimental.pallas import tpu as pltpu
from jax.sharding import PartitionSpec as P


LANES = 128
BLOCK = 256
VMEM_LIMIT = 60 * 1024 * 1024


def split_columns(blocks):
    if blocks < 5:
        return [1] * blocks
    sizes = [1]
    left = blocks - 2
    while left > 0:
        sizes.append(min(2, left))
        left -= sizes[-1]
    return sizes + [1]


def shifted_rows(row, count):
    width = row.shape[1]
    wide = jnp.broadcast_to(row, (count, width))
    return pltpu.roll(wide, 0, 1, stride=1, stride_axis=0)


def range_weights_kernel(taps, chirp_ref, weights_ref):
    filled = jnp.zeros((2, BLOCK), jnp.float32)
    padded = jnp.concatenate([chirp_ref[...].astype(jnp.float32), filled], axis=1)
    real = jnp.transpose(shifted_rows(padded[0:1], BLOCK))
    imag = jnp.transpose(shifted_rows(padded[1:2], BLOCK))
    upper = jnp.concatenate([real, -imag], axis=1)
    lower = jnp.concatenate([imag, real], axis=1)
    weights_ref[...] = jnp.concatenate([upper, lower], axis=0).astype(jnp.bfloat16)


def range_weights(chirp):
    taps = chirp.shape[1]
    return pl.pallas_call(
        functools.partial(range_weights_kernel, taps),
        out_shape=jax.ShapeDtypeStruct((4 * BLOCK, 2 * BLOCK), jnp.bfloat16),
        name="range_weights",
    )(chirp)


def range_kernel(weights_ref, here_ref, after_ref, out_ref):
    segment = jnp.concatenate([here_ref[0], after_ref[0], here_ref[1], after_ref[1]], axis=1)
    product = jnp.dot(segment, weights_ref[...], preferred_element_type=jnp.float32)
    out_ref[0] = product[:, :BLOCK].astype(out_ref.dtype)
    out_ref[1] = product[:, BLOCK:].astype(out_ref.dtype)


def range_compress(raw, beyond, weights, first, count):
    lines = raw.shape[1]
    last = raw.shape[2] // BLOCK - 1
    shape = (2, lines, BLOCK)
    if beyond is None:
        after = raw
        after_map = lambda i: (0, 0, first + i + 1)
    else:
        after = beyond
        after_map = lambda i: (0, 0, 0)
    return pl.pallas_call(
        range_kernel,
        grid=(count,),
        in_specs=[
            pl.BlockSpec(weights.shape, lambda i: (0, 0)),
            pl.BlockSpec(shape, lambda i: (0, 0, first + i)),
            pl.BlockSpec(shape, after_map),
        ],
        out_specs=pl.BlockSpec(shape, lambda i: (0, 0, i)),
        out_shape=jax.ShapeDtypeStruct((2, lines, BLOCK * count), raw.dtype),
        compiler_params=pltpu.CompilerParams(vmem_limit_bytes=VMEM_LIMIT),
        name="range_compress",
    )(weights, raw, after)


def azimuth_kernel(first, sets_ref, refs_ref, here_ref, after_ref, *rest):
    out_ref, weights_ref = rest[-2:]
    lines = here_ref.shape[1]
    set_count = refs_ref.shape[1]
    taps = refs_ref.shape[2]
    span = taps + BLOCK
    position = (first + pl.program_id(0)) * BLOCK
    for group in range(BLOCK // LANES):
        chosen = sets_ref[position + group * LANES]
        picks = lax.broadcasted_iota(jnp.int32, (8, set_count), 1) == chosen
        picks = picks.astype(jnp.bfloat16)
        for part in range(2):
            rows = jnp.dot(picks, refs_ref[part], preferred_element_type=jnp.float32)
            padded = jnp.concatenate([rows, jnp.zeros((8, 2 * BLOCK), jnp.float32)], axis=1)
            base = pltpu.roll(padded, 0, 1, stride=1, stride_axis=0)
            pieces = [base] + [pltpu.roll(base, 8 * q, 1) for q in range(1, LANES // 8)]
            top = jnp.concatenate(pieces, axis=0).astype(jnp.bfloat16)
            low = jnp.concatenate([top[:, -LANES:], top[:, : span - LANES]], axis=1)
            start = part * BLOCK
            weights_ref[start : start + LANES, :] = top[:, :span]
            weights_ref[start + LANES : start + BLOCK, :] = low
        columns = slice(group * LANES, (group + 1) * LANES)
        here = jnp.concatenate([here_ref[0, :, columns], here_ref[1, :, columns]], axis=1)
        after = jnp.concatenate([after_ref[0, :, columns], after_ref[1, :, columns]], axis=1)
        whole = jnp.concatenate([here, after], axis=0)
        for start in range(0, lines, BLOCK):
            product = jnp.dot(
                weights_ref[...], whole[start : start + span], preferred_element_type=jnp.float32
            )
            real = product[:BLOCK, :LANES] + product[BLOCK:, LANES:]
            imag = product[:BLOCK, LANES:] - product[BLOCK:, :LANES]
            out_ref[0, start : start + BLOCK, columns] = real.astype(out_ref.dtype)
            out_ref[1, start : start + BLOCK, columns] = imag.astype(out_ref.dtype)


def azimuth_compress(sets, refs, here, after, current, columns, first):
    lines = here.shape[1]
    count = here.shape[2] // BLOCK
    span = refs.shape[2] + BLOCK
    shape = (2, lines, BLOCK)
    in_specs = [
        pl.BlockSpec(refs.shape, lambda i, s: (0, 0, 0)),
        pl.BlockSpec(shape, lambda i, s: (0, 0, i)),
        pl.BlockSpec(shape, lambda i, s: (0, 0, i)),
    ]
    operands = [sets, refs, here, after]
    aliases = {}
    if current is not None:
        in_specs.append(pl.BlockSpec(memory_space=pl.ANY))
        operands.append(current)
        aliases = {4: 0}
    return pl.pallas_call(
        functools.partial(azimuth_kernel, first),
        grid_spec=pltpu.PrefetchScalarGridSpec(
            num_scalar_prefetch=1,
            grid=(count,),
            in_specs=in_specs,
            out_specs=pl.BlockSpec(shape, lambda i, s: (0, 0, first + i)),
            scratch_shapes=[pltpu.VMEM((2 * BLOCK, span), jnp.bfloat16)],
        ),
        out_shape=jax.ShapeDtypeStruct((2, lines, columns), here.dtype),
        input_output_aliases=aliases,
        compiler_params=pltpu.CompilerParams(vmem_limit_bytes=VMEM_LIMIT),
        name="azimuth_compress",
    )(*operands)


def passed_back(block, axis):
    size = lax.axis_size(axis)
    return lax.ppermute(block, axis, [(i + 1, i) for i in range(size - 1)])


def local(raw, chirp, az_ref, set_index):
    columns = raw.shape[2]
    range_taps = chirp.shape[1]
    beyond = passed_back(raw[:, :, :range_taps], "rg")
    weights = range_weights(chirp)
    sizes = split_columns(columns // BLOCK)
    starts = [sum(sizes[:k]) for k in range(len(sizes))]
    here, after = [], []
    for start, size in zip(starts, sizes):
        final = start + size == columns // BLOCK
        piece = range_compress(raw, beyond if final else None, weights, start, size)
        here.append(piece)
        after.append(passed_back(piece, "az"))
    focused = None
    for k, start in enumerate(starts):
        focused = azimuth_compress(
            set_index, az_ref, here[k], after[k], focused, columns, start
        )
    return focused


def solution(mesh):
    in_specs = (P(None, "az", "rg"), P(), P(), P("rg"))
    out_specs = P(None, "az", "rg")
    return jax.shard_map(local, mesh=mesh, in_specs=in_specs, out_specs=out_specs, check_vma=False)
```

```python
import functools

import jax
import jax.numpy as jnp
from jax import lax
from jax.experimental import pallas as pl
from jax.experimental.pallas import tpu as pltpu
from jax.sharding import PartitionSpec as P


LANES = 128
BLOCK = 256
VMEM_LIMIT = 32 * 1024 * 1024
WHOLE = pl.BlockSpec(memory_space=pltpu.VMEM)
ANYWHERE = pl.BlockSpec(memory_space=pl.ANY)


def split_columns(blocks):
    if blocks < 5:
        return [1] * blocks
    sizes = [1]
    left = blocks - 2
    while left > 0:
        sizes.append(min(2, left))
        left -= sizes[-1]
    return sizes + [1]


def shifted_rows(row, count):
    wide = jnp.broadcast_to(row, (count, row.shape[1]))
    return pltpu.roll(wide, 0, 1, stride=1, stride_axis=0)


def build_range_weights(chirp_ref, weights_ref):
    filled = jnp.zeros((2, BLOCK), jnp.float32)
    padded = jnp.concatenate([chirp_ref[...].astype(jnp.float32), filled], axis=1)
    real = jnp.transpose(shifted_rows(padded[0:1], BLOCK)).astype(jnp.bfloat16)
    imag = jnp.transpose(shifted_rows(padded[1:2], BLOCK)).astype(jnp.bfloat16)
    half = 2 * BLOCK
    weights_ref[:half, :BLOCK] = real
    weights_ref[:half, BLOCK:] = -imag
    weights_ref[half:, :BLOCK] = imag
    weights_ref[half:, BLOCK:] = real


def range_kernel(leading, final, chirp_ref, here_ref, after_ref, *rest):
    out_ref = rest[-3] if leading else rest[-2]
    weights_ref = rest[-1]
    step = pl.program_id(0)

    @pl.when(step == 0)
    def _():
        build_range_weights(chirp_ref, weights_ref)

    if leading:
        rest[-2][...] = here_ref[...]
    after = after_ref[...]
    if final:
        turn = lax.axis_size("rg") // 2
        after = jnp.where(lax.axis_index("rg") % turn == turn - 1, rest[0][...], after)
    segment = jnp.concatenate([here_ref[0], after[0], here_ref[1], after[1]], axis=1)
    product = jnp.dot(segment, weights_ref[...], preferred_element_type=jnp.float32)
    columns = pl.ds(pl.multiple_of(step * BLOCK, BLOCK), BLOCK)
    out_ref[0, :, columns] = product[:, :BLOCK].astype(out_ref.dtype)
    out_ref[1, :, columns] = product[:, BLOCK:].astype(out_ref.dtype)


def range_compress(raw, beyond, chirp, previous, first, count):
    lines = raw.shape[1]
    shape = (2, lines, BLOCK)
    final = beyond is not None
    if final:
        after = list(beyond)
        after_specs = [WHOLE, WHOLE]
    else:
        after = [raw]
        after_specs = [pl.BlockSpec(shape, lambda i: (0, 0, first + i + 1))]
    in_specs = [
        pl.BlockSpec(chirp.shape, lambda i: (0, 0)),
        pl.BlockSpec(shape, lambda i: (0, 0, first + i)),
        *after_specs,
    ]
    operands = [chirp, raw, *after]
    out_shape = [jax.ShapeDtypeStruct((2, lines, BLOCK * count), raw.dtype)]
    out_specs = [WHOLE]
    leading = previous is None
    if leading:
        out_shape.append(jax.ShapeDtypeStruct(shape, raw.dtype))
        out_specs.append(WHOLE)
    else:
        in_specs.append(ANYWHERE)
        operands.append(previous)
    return pl.pallas_call(
        functools.partial(range_kernel, leading, final),
        grid=(count,),
        in_specs=in_specs,
        out_specs=out_specs,
        out_shape=out_shape,
        scratch_shapes=[pltpu.VMEM((4 * BLOCK, 2 * BLOCK), jnp.bfloat16)],
        compiler_params=pltpu.CompilerParams(vmem_limit_bytes=VMEM_LIMIT),
        name="range_compress",
    )(*operands)


def azimuth_kernel(first, sets_ref, refs_ref, here_ref, after_ref, *rest):
    out_ref, weights_ref = rest[-2:]
    lines = here_ref.shape[1]
    set_count = refs_ref.shape[1]
    span = refs_ref.shape[2] + BLOCK
    step = pl.program_id(0)
    for group in range(BLOCK // LANES):
        offset = pl.multiple_of(step * BLOCK + group * LANES, LANES)
        chosen = sets_ref[first * BLOCK + offset]
        picks = lax.broadcasted_iota(jnp.int32, (8, set_count), 1) == chosen
        picks = picks.astype(jnp.bfloat16)
        for part in range(2):
            rows = jnp.dot(picks, refs_ref[part], preferred_element_type=jnp.float32)
            padded = jnp.concatenate([rows, jnp.zeros((8, 2 * BLOCK), jnp.float32)], axis=1)
            base = pltpu.roll(padded, 0, 1, stride=1, stride_axis=0)
            pieces = [base] + [pltpu.roll(base, 8 * q, 1) for q in range(1, LANES // 8)]
            top = jnp.concatenate(pieces, axis=0).astype(jnp.bfloat16)
            low = jnp.concatenate([top[:, -LANES:], top[:, : span - LANES]], axis=1)
            start = part * BLOCK
            weights_ref[start : start + LANES, :] = top[:, :span]
            weights_ref[start + LANES : start + BLOCK, :] = low
        at = pl.ds(offset, LANES)
        here = jnp.concatenate([here_ref[0, :, at], here_ref[1, :, at]], axis=1)
        after = jnp.concatenate([after_ref[0, :, at], after_ref[1, :, at]], axis=1)
        whole = jnp.concatenate([here, after], axis=0)
        columns = slice(group * LANES, (group + 1) * LANES)
        for start in range(0, lines, BLOCK):
            product = jnp.dot(
                weights_ref[...], whole[start : start + span], preferred_element_type=jnp.float32
            )
            real = product[:BLOCK, :LANES] + product[BLOCK:, LANES:]
            imag = product[:BLOCK, LANES:] - product[BLOCK:, :LANES]
            out_ref[0, start : start + BLOCK, columns] = real.astype(out_ref.dtype)
            out_ref[1, start : start + BLOCK, columns] = imag.astype(out_ref.dtype)


def azimuth_compress(sets, refs, here, after, current, columns, first):
    lines = here.shape[1]
    count = here.shape[2] // BLOCK
    span = refs.shape[2] + BLOCK
    in_specs = [pl.BlockSpec(refs.shape, lambda i, s: (0, 0, 0)), WHOLE, WHOLE]
    operands = [sets, refs, here, after]
    aliases = {}
    if current is not None:
        in_specs.append(ANYWHERE)
        operands.append(current)
        aliases = {4: 0}
    return pl.pallas_call(
        functools.partial(azimuth_kernel, first),
        grid_spec=pltpu.PrefetchScalarGridSpec(
            num_scalar_prefetch=1,
            grid=(count,),
            in_specs=in_specs,
            out_specs=pl.BlockSpec((2, lines, BLOCK), lambda i, s: (0, 0, first + i)),
            scratch_shapes=[pltpu.VMEM((2 * BLOCK, span), jnp.bfloat16)],
        ),
        out_shape=jax.ShapeDtypeStruct((2, lines, columns), here.dtype),
        input_output_aliases=aliases,
        compiler_params=pltpu.CompilerParams(vmem_limit_bytes=VMEM_LIMIT),
        name="azimuth_compress",
    )(*operands)


def passed_back(block, axis):
    size = lax.axis_size(axis)
    return lax.ppermute(block, axis, [(i + 1, i) for i in range(size - 1)])


def edge_routes(az_size, rg_size):
    upper, turn = az_size // 2, rg_size // 2
    flat = lambda i, j: i * rg_size + j
    first, second = [], []
    for i in range(az_size):
        for j in range(rg_size - 1):
            if j != turn - 1:
                first.append((flat(i, j + 1), flat(i, j)))
            elif i < upper:
                first.append((flat(i, turn), flat(i + upper, rg_size - 1)))
                second.append((flat(i + upper, rg_size - 1), flat(i, j)))
            else:
                first.append((flat(i, turn), flat(i - upper, j)))
                second.append((flat(i - upper, j), flat(i, j)))
    return first, second


def local(raw, chirp, az_ref, set_index):
    columns = raw.shape[2]
    blocks = columns // BLOCK
    sizes = split_columns(blocks)
    starts = [sum(sizes[:k]) for k in range(len(sizes))]
    axes = ("az", "rg")
    first_route, second_route = edge_routes(lax.axis_size("az"), lax.axis_size("rg"))
    here, after = [], []
    previous, beyond = None, None
    raw = pltpu.with_memory_space_constraint(raw, pltpu.HBM)
    for start, size in zip(starts, sizes):
        final = start + size == blocks
        made = range_compress(raw, beyond if final else None, chirp, previous, start, size)
        previous = made[0]
        here.append(previous)
        after.append(passed_back(previous, "az"))
        if start == 0:
            near = lax.ppermute(made[1], axes, first_route)
            far = lax.ppermute(near, axes, second_route)
            beyond = (near, far)
    focused = None
    for k, start in enumerate(starts):
        focused = azimuth_compress(
            set_index, az_ref, here[k], after[k], focused, columns, start
        )
    return focused


def solution(mesh):
    in_specs = (P(None, "az", "rg"), P(), P(), P("rg"))
    out_specs = P(None, "az", "rg")
    return jax.shard_map(local, mesh=mesh, in_specs=in_specs, out_specs=out_specs, check_vma=False)
```

```python
import functools

import jax
import jax.numpy as jnp
from jax import lax
from jax.experimental import pallas as pl
from jax.experimental.pallas import tpu as pltpu
from jax.sharding import PartitionSpec as P


LANES = 128
BLOCK = 256
HEAD_ROWS = 128
VMEM_LIMIT = 16 * 1024 * 1024
WHOLE = pl.BlockSpec(memory_space=pltpu.VMEM)
ANYWHERE = pl.BlockSpec(memory_space=pl.ANY)
PARAMS = pltpu.CompilerParams(vmem_limit_bytes=VMEM_LIMIT)


def shifted_rows(row, count):
    wide = jnp.broadcast_to(row, (count, row.shape[1]))
    return pltpu.roll(wide, 0, 1, stride=1, stride_axis=0)


def build_range_weights(chirp_ref, weights_ref):
    filled = jnp.zeros((2, BLOCK), jnp.float32)
    padded = jnp.concatenate([chirp_ref[...].astype(jnp.float32), filled], axis=1)
    real = jnp.transpose(shifted_rows(padded[0:1], BLOCK)).astype(jnp.bfloat16)
    imag = jnp.transpose(shifted_rows(padded[1:2], BLOCK)).astype(jnp.bfloat16)
    half = 2 * BLOCK
    weights_ref[:half, :BLOCK] = real
    weights_ref[:half, BLOCK:] = -imag
    weights_ref[half:, :BLOCK] = imag
    weights_ref[half:, BLOCK:] = real


def correlate(segment, weights_ref):
    product = jnp.dot(segment, weights_ref[...], preferred_element_type=jnp.float32)
    product = product.astype(jnp.bfloat16)
    return product[:, :BLOCK], product[:, BLOCK:]


def head_kernel(chirp_ref, raw_ref, out_ref, weights_ref):
    step = pl.program_id(0)

    @pl.when(step == 0)
    def _():
        build_range_weights(chirp_ref, weights_ref)

    segment = jnp.concatenate([raw_ref[0], raw_ref[1]], axis=1)
    rows = pl.ds(pl.multiple_of(step * HEAD_ROWS, HEAD_ROWS), HEAD_ROWS)
    out_ref[0, rows], out_ref[1, rows] = correlate(segment, weights_ref)


def range_head(raw, chirp):
    lines = raw.shape[1]
    return pl.pallas_call(
        head_kernel,
        grid=(lines // HEAD_ROWS,),
        in_specs=[
            pl.BlockSpec(chirp.shape, lambda i: (0, 0)),
            pl.BlockSpec((2, HEAD_ROWS, 2 * BLOCK), lambda i: (0, i, 0)),
        ],
        out_specs=[WHOLE, WHOLE],
        out_shape=[
            jax.ShapeDtypeStruct((2, lines, BLOCK), raw.dtype),
            jax.ShapeDtypeStruct((4 * BLOCK, 2 * BLOCK), raw.dtype),
        ],
        compiler_params=PARAMS,
        name="range_head",
    )(chirp, raw)


def range_kernel(first, sizes, with_edge, weights_ref, raw_ref, *rest):
    outs = rest[-len(sizes) - with_edge :]
    if with_edge:
        outs[-1][...] = raw_ref[:, :, :BLOCK]
    block = first
    for out_ref, size in zip(outs, sizes):
        for k in range(size):
            span = slice(block * BLOCK, (block + 2) * BLOCK)
            segment = jnp.concatenate([raw_ref[0, :, span], raw_ref[1, :, span]], axis=1)
            columns = slice(k * BLOCK, (k + 1) * BLOCK)
            out_ref[0, :, columns], out_ref[1, :, columns] = correlate(segment, weights_ref)
            block += 1


def range_compress(raw, weights, previous, first, sizes, with_edge):
    lines = raw.shape[1]
    widths = [BLOCK * size for size in sizes] + [BLOCK] * with_edge
    return pl.pallas_call(
        functools.partial(range_kernel, first, sizes, with_edge),
        in_specs=[WHOLE, WHOLE, ANYWHERE],
        out_specs=[WHOLE] * len(widths),
        out_shape=[jax.ShapeDtypeStruct((2, lines, width), raw.dtype) for width in widths],
        compiler_params=PARAMS,
        name="range_compress",
    )(weights, raw, previous)


def tail_kernel(weights_ref, raw_ref, near_ref, far_ref, out_ref):
    turn = lax.axis_size("rg") // 2
    crossing = lax.axis_index("rg") % turn == turn - 1
    after = jnp.where(crossing, far_ref[...], near_ref[...])
    here = raw_ref[:, :, raw_ref.shape[2] - BLOCK :]
    segment = jnp.concatenate([here[0], after[0], here[1], after[1]], axis=1)
    out_ref[0], out_ref[1] = correlate(segment, weights_ref)


def range_tail(raw, weights, near, far):
    return pl.pallas_call(
        tail_kernel,
        in_specs=[WHOLE] * 4,
        out_specs=WHOLE,
        out_shape=jax.ShapeDtypeStruct((2, raw.shape[1], BLOCK), raw.dtype),
        compiler_params=PARAMS,
        name="range_tail",
    )(weights, raw, near, far)


def azimuth_weights_kernel(sets_ref, refs_ref, previous_ref, weights_ref, wide_ref):
    taps = refs_ref.shape[2]
    span = taps + BLOCK
    group = pl.program_id(0)

    @pl.when(group == 0)
    def _():
        wide_ref[...] = refs_ref[...].astype(jnp.float32)

    chosen = sets_ref[group * LANES]
    for part in range(2):
        row = wide_ref[part, pl.ds(chosen, 1), :]
        padded = jnp.concatenate([row, jnp.zeros((1, 2 * BLOCK), jnp.float32)], axis=1)
        base = shifted_rows(padded, 8)
        start = part * BLOCK
        for q in range(0, LANES, 16):
            upper = pltpu.roll(base, q, 1) if q else base
            lower = pltpu.roll(base, q + 8, 1)
            top = jnp.concatenate([upper, lower], axis=0).astype(jnp.bfloat16)
            low = jnp.concatenate([top[:, -LANES:], top[:, : span - LANES]], axis=1)
            weights_ref[group, start + q : start + q + 16, :] = top[:, :span]
            weights_ref[group, start + LANES + q : start + LANES + q + 16, :] = low


def azimuth_weights(sets, refs, previous):
    taps = refs.shape[2]
    groups = sets.shape[0] // LANES
    return pl.pallas_call(
        azimuth_weights_kernel,
        grid_spec=pltpu.PrefetchScalarGridSpec(
            num_scalar_prefetch=1,
            grid=(groups,),
            in_specs=[WHOLE, ANYWHERE],
            out_specs=WHOLE,
            scratch_shapes=[pltpu.VMEM(refs.shape, jnp.float32)],
        ),
        out_shape=jax.ShapeDtypeStruct((groups, 2 * BLOCK, taps + BLOCK), refs.dtype),
        compiler_params=PARAMS,
        name="azimuth_weights",
    )(sets, refs, previous)


def azimuth_kernel(first, weights_ref, here_ref, after_ref, *rest):
    out_ref = rest[-1]
    lines = here_ref.shape[1]
    span = weights_ref.shape[2]
    step = pl.program_id(0)
    for group in range(BLOCK // LANES):
        at = pl.ds(pl.multiple_of(step * BLOCK + group * LANES, LANES), LANES)
        here = jnp.concatenate([here_ref[0, :, at], here_ref[1, :, at]], axis=1)
        after = jnp.concatenate([after_ref[0, :, at], after_ref[1, :, at]], axis=1)
        whole = jnp.concatenate([here, after], axis=0)
        weights = weights_ref[(first + step) * (BLOCK // LANES) + group]
        columns = slice(group * LANES, (group + 1) * LANES)
        for start in range(0, lines, BLOCK):
            product = jnp.dot(
                weights, whole[start : start + span], preferred_element_type=jnp.float32
            )
            real = product[:BLOCK, :LANES] + product[BLOCK:, LANES:]
            imag = product[:BLOCK, LANES:] - product[BLOCK:, :LANES]
            out_ref[0, start : start + BLOCK, columns] = real.astype(out_ref.dtype)
            out_ref[1, start : start + BLOCK, columns] = imag.astype(out_ref.dtype)


def azimuth_compress(weights, here, after, current, columns, first):
    lines = here.shape[1]
    count = here.shape[2] // BLOCK
    in_specs = [WHOLE, WHOLE, WHOLE]
    operands = [weights, here, after]
    aliases = {}
    if current is not None:
        in_specs.append(ANYWHERE)
        operands.append(current)
        aliases = {3: 0}
    return pl.pallas_call(
        functools.partial(azimuth_kernel, first),
        grid=(count,),
        in_specs=in_specs,
        out_specs=pl.BlockSpec((2, lines, BLOCK), lambda i: (0, 0, first + i)),
        out_shape=jax.ShapeDtypeStruct((2, lines, columns), here.dtype),
        input_output_aliases=aliases,
        compiler_params=PARAMS,
        name="azimuth_compress",
    )(*operands)


def passed_back(block, axis):
    size = lax.axis_size(axis)
    return lax.ppermute(block, axis, [(i + 1, i) for i in range(size - 1)])


def edge_routes(az_size, rg_size):
    upper, turn = az_size // 2, rg_size // 2
    flat = lambda i, j: i * rg_size + j
    first, second = [], []
    for i in range(az_size):
        for j in range(rg_size - 1):
            if j != turn - 1:
                first.append((flat(i, j + 1), flat(i, j)))
            elif i < upper:
                first.append((flat(i, turn), flat(i + upper, rg_size - 1)))
                second.append((flat(i + upper, rg_size - 1), flat(i, j)))
            else:
                first.append((flat(i, turn), flat(i - upper, j)))
                second.append((flat(i - upper, j), flat(i, j)))
    return first, second


def local(raw, chirp, az_ref, set_index):
    columns = raw.shape[2]
    axes = ("az", "rg")
    first_route, second_route = edge_routes(lax.axis_size("az"), lax.axis_size("rg"))
    distant = pltpu.with_memory_space_constraint(raw, pltpu.HBM)
    first, weights = range_head(
        distant, pltpu.with_memory_space_constraint(chirp, pltpu.HBM)
    )
    second, edge = range_compress(raw, weights, first, 1, (2,), True)
    third, fourth = range_compress(raw, weights, second, 3, (2, 2), False)
    here = [first, second, third, fourth]
    after = []
    for piece in here:
        after.append(passed_back(piece, "az"))
    near = lax.ppermute(edge, axes, first_route)
    far = lax.ppermute(near, axes, second_route)
    here.append(range_tail(raw, weights, near, far))
    after.append(passed_back(here[-1], "az"))
    turns = azimuth_weights(set_index, az_ref, third)
    focused = None
    start = 0
    for k, piece in enumerate(here):
        focused = azimuth_compress(turns, piece, after[k], focused, columns, start)
        start += piece.shape[2] // BLOCK
    return focused


def solution(mesh):
    in_specs = (P(None, "az", "rg"), P(), P(), P("rg"))
    out_specs = P(None, "az", "rg")
    return jax.shard_map(local, mesh=mesh, in_specs=in_specs, out_specs=out_specs, check_vma=False)
```

```python
import functools

import jax
import jax.numpy as jnp
from jax import lax
from jax.experimental import pallas as pl
from jax.experimental.pallas import tpu as pltpu
from jax.sharding import PartitionSpec as P


LANES = 128
BLOCK = 256
HEAD_ROWS = 128
VMEM_LIMIT = 16 * 1024 * 1024
WHOLE = pl.BlockSpec(memory_space=pltpu.VMEM)
ANYWHERE = pl.BlockSpec(memory_space=pl.ANY)
PARAMS = pltpu.CompilerParams(vmem_limit_bytes=VMEM_LIMIT)


def shifted_rows(row, count):
    wide = jnp.broadcast_to(row, (count, row.shape[1]))
    return pltpu.roll(wide, 0, 1, stride=1, stride_axis=0)


def build_range_weights(chirp_ref, weights_ref):
    filled = jnp.zeros((2, BLOCK), jnp.float32)
    padded = jnp.concatenate([chirp_ref[...].astype(jnp.float32), filled], axis=1)
    real = jnp.transpose(shifted_rows(padded[0:1], BLOCK)).astype(jnp.bfloat16)
    imag = jnp.transpose(shifted_rows(padded[1:2], BLOCK)).astype(jnp.bfloat16)
    half = 2 * BLOCK
    weights_ref[:half, :BLOCK] = real
    weights_ref[:half, BLOCK:] = -imag
    weights_ref[half:, :BLOCK] = imag
    weights_ref[half:, BLOCK:] = real


def correlate(segment, weights_ref):
    product = jnp.dot(segment, weights_ref[...], preferred_element_type=jnp.float32)
    product = product.astype(jnp.bfloat16)
    return product[:, :BLOCK], product[:, BLOCK:]


def head_kernel(chirp_ref, raw_ref, out_ref, weights_ref):
    step = pl.program_id(0)

    @pl.when(step == 0)
    def _():
        build_range_weights(chirp_ref, weights_ref)

    segment = jnp.concatenate([raw_ref[0], raw_ref[1]], axis=1)
    rows = pl.ds(pl.multiple_of(step * HEAD_ROWS, HEAD_ROWS), HEAD_ROWS)
    out_ref[0, rows], out_ref[1, rows] = correlate(segment, weights_ref)


def range_head(raw, chirp):
    lines = raw.shape[1]
    return pl.pallas_call(
        head_kernel,
        grid=(lines // HEAD_ROWS,),
        in_specs=[
            pl.BlockSpec(chirp.shape, lambda i: (0, 0)),
            pl.BlockSpec((2, HEAD_ROWS, 2 * BLOCK), lambda i: (0, i, 0)),
        ],
        out_specs=[WHOLE, WHOLE],
        out_shape=[
            jax.ShapeDtypeStruct((2, lines, BLOCK), raw.dtype),
            jax.ShapeDtypeStruct((4 * BLOCK, 2 * BLOCK), raw.dtype),
        ],
        compiler_params=PARAMS,
        name="range_head",
    )(chirp, raw)


def range_kernel(first, sizes, with_edge, weights_ref, raw_ref, *rest):
    outs = rest[-len(sizes) - with_edge :]
    if with_edge:
        outs[-1][...] = raw_ref[:, :, :BLOCK]
    block = first
    for out_ref, size in zip(outs, sizes):
        for k in range(size):
            span = slice(block * BLOCK, (block + 2) * BLOCK)
            segment = jnp.concatenate([raw_ref[0, :, span], raw_ref[1, :, span]], axis=1)
            columns = slice(k * BLOCK, (k + 1) * BLOCK)
            out_ref[0, :, columns], out_ref[1, :, columns] = correlate(segment, weights_ref)
            block += 1


def range_compress(raw, weights, previous, first, sizes, with_edge):
    lines = raw.shape[1]
    widths = [BLOCK * size for size in sizes] + [BLOCK] * with_edge
    return pl.pallas_call(
        functools.partial(range_kernel, first, sizes, with_edge),
        in_specs=[WHOLE, WHOLE, ANYWHERE],
        out_specs=[WHOLE] * len(widths),
        out_shape=[jax.ShapeDtypeStruct((2, lines, width), raw.dtype) for width in widths],
        compiler_params=PARAMS,
        name="range_compress",
    )(weights, raw, previous)


def tail_kernel(weights_ref, raw_ref, near_ref, far_ref, out_ref):
    turn = lax.axis_size("rg") // 2
    crossing = lax.axis_index("rg") % turn == turn - 1
    after = jnp.where(crossing, far_ref[...], near_ref[...])
    here = raw_ref[:, :, raw_ref.shape[2] - BLOCK :]
    segment = jnp.concatenate([here[0], after[0], here[1], after[1]], axis=1)
    out_ref[0], out_ref[1] = correlate(segment, weights_ref)


def range_tail(raw, weights, near, far):
    return pl.pallas_call(
        tail_kernel,
        in_specs=[WHOLE] * 4,
        out_specs=WHOLE,
        out_shape=jax.ShapeDtypeStruct((2, raw.shape[1], BLOCK), raw.dtype),
        compiler_params=PARAMS,
        name="range_tail",
    )(weights, raw, near, far)


def azimuth_weights_kernel(sets_ref, refs_ref, previous_ref, weights_ref, wide_ref):
    taps = refs_ref.shape[2]
    span = taps + BLOCK
    group = pl.program_id(0)

    @pl.when(group == 0)
    def _():
        wide_ref[...] = refs_ref[...].astype(jnp.float32)

    chosen = sets_ref[group * LANES]
    for part in range(2):
        row = wide_ref[part, pl.ds(chosen, 1), :]
        padded = jnp.concatenate([row, jnp.zeros((1, 2 * BLOCK), jnp.float32)], axis=1)
        base = shifted_rows(padded, 8)
        start = part * BLOCK
        for q in range(0, LANES, 16):
            upper = pltpu.roll(base, q, 1) if q else base
            lower = pltpu.roll(base, q + 8, 1)
            top = jnp.concatenate([upper, lower], axis=0).astype(jnp.bfloat16)
            low = jnp.concatenate([top[:, -LANES:], top[:, : span - LANES]], axis=1)
            weights_ref[group, start + q : start + q + 16, :] = top[:, :span]
            weights_ref[group, start + LANES + q : start + LANES + q + 16, :] = low


def azimuth_weights(sets, refs, previous):
    taps = refs.shape[2]
    groups = sets.shape[0] // LANES
    return pl.pallas_call(
        azimuth_weights_kernel,
        grid_spec=pltpu.PrefetchScalarGridSpec(
            num_scalar_prefetch=1,
            grid=(groups,),
            in_specs=[WHOLE, ANYWHERE],
            out_specs=WHOLE,
            scratch_shapes=[pltpu.VMEM(refs.shape, jnp.float32)],
        ),
        out_shape=jax.ShapeDtypeStruct((groups, 2 * BLOCK, taps + BLOCK), refs.dtype),
        compiler_params=PARAMS,
        name="azimuth_weights",
    )(sets, refs, previous)


def azimuth_kernel(first, relayed, weights_ref, here_ref, after_ref, *rest):
    out_ref = rest[-1]
    by_relay = lax.axis_index("az") % 2 == 1
    lines = here_ref.shape[1]
    span = weights_ref.shape[2]
    step = pl.program_id(0)
    for group in range(BLOCK // LANES):
        at = pl.ds(pl.multiple_of(step * BLOCK + group * LANES, LANES), LANES)
        here = jnp.concatenate([here_ref[0, :, at], here_ref[1, :, at]], axis=1)
        after = jnp.concatenate([after_ref[0, :, at], after_ref[1, :, at]], axis=1)
        if relayed:
            other = jnp.concatenate([rest[0][0, :, at], rest[0][1, :, at]], axis=1)
            after = jnp.where(by_relay, other, after)
        whole = jnp.concatenate([here, after], axis=0)
        weights = weights_ref[(first + step) * (BLOCK // LANES) + group]
        columns = slice(group * LANES, (group + 1) * LANES)
        for start in range(0, lines, BLOCK):
            product = jnp.dot(
                weights, whole[start : start + span], preferred_element_type=jnp.float32
            )
            real = product[:BLOCK, :LANES] + product[BLOCK:, LANES:]
            imag = product[:BLOCK, LANES:] - product[BLOCK:, :LANES]
            out_ref[0, start : start + BLOCK, columns] = real.astype(out_ref.dtype)
            out_ref[1, start : start + BLOCK, columns] = imag.astype(out_ref.dtype)


def azimuth_compress(weights, here, after, current, columns, first):
    lines = here.shape[1]
    count = here.shape[2] // BLOCK
    operands = [weights, here, *after]
    in_specs = [WHOLE] * len(operands)
    aliases = {}
    if current is not None:
        aliases = {len(operands): 0}
        in_specs.append(ANYWHERE)
        operands.append(current)
    return pl.pallas_call(
        functools.partial(azimuth_kernel, first, len(after) > 1),
        grid=(count,),
        in_specs=in_specs,
        out_specs=pl.BlockSpec((2, lines, BLOCK), lambda i: (0, 0, first + i)),
        out_shape=jax.ShapeDtypeStruct((2, lines, columns), here.dtype),
        input_output_aliases=aliases,
        compiler_params=PARAMS,
        name="azimuth_compress",
    )(*operands)


def passed_back(block, axis):
    size = lax.axis_size(axis)
    return lax.ppermute(block, axis, [(i + 1, i) for i in range(size - 1)])


def edge_routes(az_size, rg_size):
    upper, turn = az_size // 2, rg_size // 2
    flat = lambda i, j: i * rg_size + j
    first, second = [], []
    for i in range(az_size):
        for j in range(rg_size - 1):
            if j != turn - 1:
                first.append((flat(i, j + 1), flat(i, j)))
            elif i < upper:
                first.append((flat(i, turn), flat(i + upper, rg_size - 1)))
                second.append((flat(i + upper, rg_size - 1), flat(i, j)))
            else:
                first.append((flat(i, turn), flat(i - upper, j)))
                second.append((flat(i - upper, j), flat(i, j)))
    return first, second


def relay_routes(az_size):
    upper = az_size // 2
    ring = upper // 2
    at = lambda z, x, core: z * upper + (x % ring) * 2 + core
    hops = [[], [], []]
    for z in range(2):
        for x in range(ring):
            hops[0].append((at(z, x, 1), at(z, x, 0)))
            if x == 0 and z == 0:
                continue
            to = z if x else z - 1
            hops[0].append((at(z, x, 0), at(to, x + 1, 1)))
            hops[1].append((at(to, x + 1, 1), at(to, x + 2, 1)))
            hops[2].append((at(to, x + 2, 1), at(to, x + 3, 1)))
    return hops


def local(raw, chirp, az_ref, set_index):
    columns = raw.shape[2]
    axes = ("az", "rg")
    first_route, second_route = edge_routes(lax.axis_size("az"), lax.axis_size("rg"))
    hops = relay_routes(lax.axis_size("az"))
    first, weights = range_head(
        pltpu.with_memory_space_constraint(raw, pltpu.HBM),
        pltpu.with_memory_space_constraint(chirp, pltpu.HBM),
    )
    raw, weights = lax.optimization_barrier((raw, weights))
    turned, second, edge = range_compress(raw, weights, first, 1, (1, 2), True)
    (third,) = range_compress(raw, weights, second, 4, (3,), False)
    first_next = passed_back(first, "az")
    second_next = passed_back(second, "az")
    third_next = passed_back(third, "az")
    near = lax.ppermute(edge, axes, first_route)
    far = lax.ppermute(near, axes, second_route)
    carried = [turned]
    for hop in hops:
        carried.append(lax.ppermute(carried[-1], "az", hop))
    fourth = range_tail(raw, weights, near, far)
    fourth_next = passed_back(fourth, "az")
    turns = azimuth_weights(set_index, az_ref, third)
    focused = None
    pieces = [
        (first, [first_next], 0),
        (second, [second_next], 2),
        (third, [third_next], 4),
        (turned, [carried[1], carried[3]], 1),
        (fourth, [fourth_next], 7),
    ]
    for here, after, start in pieces:
        focused = azimuth_compress(turns, here, after, focused, columns, start)
    return focused


def solution(mesh):
    in_specs = (P(None, "az", "rg"), P(), P(), P("rg"))
    out_specs = P(None, "az", "rg")
    return jax.shard_map(local, mesh=mesh, in_specs=in_specs, out_specs=out_specs, check_vma=False)
```

```python
import functools

import jax
import jax.numpy as jnp
from jax import lax
from jax.experimental import pallas as pl
from jax.experimental.pallas import tpu as pltpu
from jax.sharding import PartitionSpec as P


LANES = 128
BLOCK = 256
TURNS = 4
VMEM_LIMIT = 16 * 1024 * 1024
WHOLE = pl.BlockSpec(memory_space=pltpu.VMEM)
ANYWHERE = pl.BlockSpec(memory_space=pl.ANY)
PARAMS = pltpu.CompilerParams(vmem_limit_bytes=VMEM_LIMIT)


def shifted_rows(row, count):
    wide = jnp.broadcast_to(row, (count, row.shape[1]))
    return pltpu.roll(wide, 0, 1, stride=1, stride_axis=0)


def build_range_weights(chirp_ref, weights_ref):
    filled = jnp.zeros((2, BLOCK), jnp.float32)
    padded = jnp.concatenate([chirp_ref[...].astype(jnp.float32), filled], axis=1)
    real = jnp.transpose(shifted_rows(padded[0:1], BLOCK)).astype(jnp.bfloat16)
    imag = jnp.transpose(shifted_rows(padded[1:2], BLOCK)).astype(jnp.bfloat16)
    half = 2 * BLOCK
    weights_ref[:half, :BLOCK] = real
    weights_ref[:half, BLOCK:] = -imag
    weights_ref[half:, :BLOCK] = imag
    weights_ref[half:, BLOCK:] = real


def correlate(segment, weights_ref):
    product = jnp.dot(segment, weights_ref[...], preferred_element_type=jnp.float32)
    product = product.astype(jnp.bfloat16)
    return product[:, :BLOCK], product[:, BLOCK:]


def block_at(ref, first, count=1):
    return ref.at[:, :, pl.ds(first * BLOCK, count * BLOCK)]


def head_kernel(
    chirp_hbm, raw_hbm, out_ref, edge_ref, kept_ref, weights_ref, chirp_ref, sems
):
    sources = [chirp_hbm, block_at(raw_hbm, 0)]
    targets = [chirp_ref, edge_ref]
    for k in range(kept_ref.shape[2] // BLOCK):
        sources.append(block_at(raw_hbm, k + 1))
        targets.append(block_at(kept_ref, k))
    copies = [
        pltpu.make_async_copy(source, target, sems.at[k])
        for k, (source, target) in enumerate(zip(sources, targets))
    ]
    for copy in copies:
        copy.start()
    copies[0].wait()
    build_range_weights(chirp_ref, weights_ref)
    copies[1].wait()
    copies[2].wait()
    after = kept_ref[:, :, :BLOCK]
    segment = jnp.concatenate([edge_ref[0], after[0], edge_ref[1], after[1]], axis=1)
    out_ref[0], out_ref[1] = correlate(segment, weights_ref)
    for copy in copies[3:]:
        copy.wait()


def range_head(raw, chirp, kept):
    lines = raw.shape[1]
    like = lambda *shape: jax.ShapeDtypeStruct(shape, raw.dtype)
    out_shape = [
        like(2, lines, BLOCK),
        like(2, lines, BLOCK),
        like(2, lines, kept * BLOCK),
        like(4 * BLOCK, 2 * BLOCK),
    ]
    return pl.pallas_call(
        head_kernel,
        in_specs=[ANYWHERE, ANYWHERE],
        out_specs=[WHOLE] * len(out_shape),
        out_shape=out_shape,
        scratch_shapes=[
            pltpu.VMEM(chirp.shape, chirp.dtype),
            pltpu.SemaphoreType.DMA((2 + kept,)),
        ],
        compiler_params=PARAMS,
        name="range_head",
    )(chirp, raw)


def range_blocks(sizes, blocks, weights_ref, outs):
    block = 0
    for out_ref, size in zip(outs, sizes):
        for k in range(size):
            here_ref, here = blocks[block]
            after_ref, after = blocks[block + 1]
            here = slice(here * BLOCK, (here + 1) * BLOCK)
            after = slice(after * BLOCK, (after + 1) * BLOCK)
            parts = []
            for part in range(2):
                parts += [here_ref[part, :, here], after_ref[part, :, after]]
            real, imag = correlate(jnp.concatenate(parts, axis=1), weights_ref)
            columns = slice(k * BLOCK, (k + 1) * BLOCK)
            out_ref[0, :, columns] = real
            out_ref[1, :, columns] = imag
            block += 1


def fetch_kernel(sizes, weights_ref, near_ref, raw_hbm, previous_ref, *refs):
    outs, kept_ref, sems = refs[: len(sizes)], refs[-2], refs[-1]
    count = kept_ref.shape[2] // BLOCK
    total = raw_hbm.shape[2] // BLOCK
    copies = [
        pltpu.make_async_copy(
            block_at(raw_hbm, total - count + k), block_at(kept_ref, k), sems.at[k]
        )
        for k in range(count)
    ]
    for copy in copies:
        copy.start()
    blocks = [(near_ref, k) for k in range(sum(sizes) + 1)]
    range_blocks(sizes, blocks, weights_ref, outs)
    for copy in copies:
        copy.wait()


def range_fetch(raw, weights, near, previous, sizes, kept):
    lines = raw.shape[1]
    widths = [BLOCK * size for size in sizes] + [BLOCK * kept]
    return pl.pallas_call(
        functools.partial(fetch_kernel, sizes),
        in_specs=[WHOLE, WHOLE, ANYWHERE, ANYWHERE],
        out_specs=[WHOLE] * len(widths),
        out_shape=[jax.ShapeDtypeStruct((2, lines, width), raw.dtype) for width in widths],
        scratch_shapes=[pltpu.SemaphoreType.DMA((kept,))],
        compiler_params=PARAMS,
        name="range_fetch",
    )(weights, near, raw, previous)


def range_kernel(size, weights_ref, near_ref, kept_ref, previous_ref, out_ref):
    last = near_ref.shape[2] // BLOCK - 1
    blocks = [(near_ref, last)] + [(kept_ref, k) for k in range(size)]
    range_blocks((size,), blocks, weights_ref, [out_ref])


def range_compress(near, kept, weights, previous, size):
    lines = near.shape[1]
    return pl.pallas_call(
        functools.partial(range_kernel, size),
        in_specs=[WHOLE, WHOLE, WHOLE, ANYWHERE],
        out_specs=WHOLE,
        out_shape=jax.ShapeDtypeStruct((2, lines, BLOCK * size), near.dtype),
        compiler_params=PARAMS,
        name="range_compress",
    )(weights, near, kept, previous)


def tail_kernel(weights_ref, kept_ref, near_ref, far_ref, out_ref):
    crossing = jnp.logical_and(
        lax.axis_index("rg") == lax.axis_size("rg") // 2 - 1,
        lax.axis_index("az") >= lax.axis_size("az") - 2,
    )
    here = kept_ref[:, :, kept_ref.shape[2] - BLOCK :]
    after = jnp.where(crossing, far_ref[...], near_ref[...])
    segment = jnp.concatenate([here[0], after[0], here[1], after[1]], axis=1)
    out_ref[0], out_ref[1] = correlate(segment, weights_ref)


def range_tail(kept, weights, near, far):
    return pl.pallas_call(
        tail_kernel,
        in_specs=[WHOLE] * 4,
        out_specs=WHOLE,
        out_shape=jax.ShapeDtypeStruct((2, kept.shape[1], BLOCK), kept.dtype),
        compiler_params=PARAMS,
        name="range_tail",
    )(weights, kept, near, far)


def azimuth_weights_kernel(sets_ref, refs_ref, previous_ref, weights_ref, wide_ref):
    width = weights_ref.shape[2]
    lead = jnp.zeros((1, LANES), jnp.float32)
    filled = jnp.zeros((1, 2 * BLOCK - LANES), jnp.float32)

    @pl.when(pl.program_id(0) == 0)
    def _():
        wide_ref[...] = refs_ref[...].astype(jnp.float32)

    for k in range(TURNS):
        group = pl.program_id(0) * TURNS + k
        chosen = sets_ref[group * LANES]
        for part in range(2):
            row = wide_ref[part, pl.ds(chosen, 1), :]
            base = shifted_rows(jnp.concatenate([lead, row, filled], axis=1), 8)
            start = part * LANES
            for q in range(0, LANES, 16):
                upper = pltpu.roll(base, q, 1) if q else base
                lower = pltpu.roll(base, q + 8, 1)
                both = jnp.concatenate([upper, lower], axis=0).astype(jnp.bfloat16)
                weights_ref[group, start + q : start + q + 16, :] = both[:, :width]


def azimuth_weights(sets, refs, previous):
    taps = refs.shape[2]
    groups = sets.shape[0] // LANES
    return pl.pallas_call(
        azimuth_weights_kernel,
        grid_spec=pltpu.PrefetchScalarGridSpec(
            num_scalar_prefetch=1,
            grid=(groups // TURNS,),
            in_specs=[WHOLE, ANYWHERE],
            out_specs=WHOLE,
            scratch_shapes=[pltpu.VMEM(refs.shape, jnp.float32)],
        ),
        out_shape=jax.ShapeDtypeStruct((groups, 2 * LANES, taps + BLOCK + LANES), refs.dtype),
        compiler_params=PARAMS,
        name="azimuth_weights",
    )(sets, refs, previous)


def azimuth_kernel(first, relayed, weights_ref, here_ref, after_ref, *rest):
    out_ref = rest[-1]
    by_relay = lax.axis_index("az") % 2 == 1
    lines = here_ref.shape[1]
    span = weights_ref.shape[2] - LANES
    step = pl.program_id(0)
    for group in range(BLOCK // LANES):
        at = pl.ds(pl.multiple_of(step * BLOCK + group * LANES, LANES), LANES)
        here = jnp.concatenate([here_ref[0, :, at], here_ref[1, :, at]], axis=1)
        after = jnp.concatenate([after_ref[0, :, at], after_ref[1, :, at]], axis=1)
        if relayed:
            other = jnp.concatenate([rest[0][0, :, at], rest[0][1, :, at]], axis=1)
            after = jnp.where(by_relay, other, after)
        whole = jnp.concatenate([here, after], axis=0)
        place = (first + step) * (BLOCK // LANES) + group
        weights = jnp.concatenate(
            [
                weights_ref[place, part * LANES : (part + 1) * LANES, lead : lead + span]
                for part in range(2)
                for lead in (LANES, 0)
            ],
            axis=0,
        )
        columns = slice(group * LANES, (group + 1) * LANES)
        for start in range(0, lines, BLOCK):
            product = jnp.dot(
                weights, whole[start : start + span], preferred_element_type=jnp.float32
            )
            real = product[:BLOCK, :LANES] + product[BLOCK:, LANES:]
            imag = product[:BLOCK, LANES:] - product[BLOCK:, :LANES]
            out_ref[0, start : start + BLOCK, columns] = real.astype(out_ref.dtype)
            out_ref[1, start : start + BLOCK, columns] = imag.astype(out_ref.dtype)


def azimuth_compress(weights, here, after, current, columns, first):
    lines = here.shape[1]
    count = here.shape[2] // BLOCK
    operands = [weights, here, *after]
    in_specs = [WHOLE] * len(operands)
    aliases = {}
    if current is not None:
        aliases = {len(operands): 0}
        in_specs.append(ANYWHERE)
        operands.append(current)
    return pl.pallas_call(
        functools.partial(azimuth_kernel, first, len(after) > 1),
        grid=(count,),
        in_specs=in_specs,
        out_specs=pl.BlockSpec((2, lines, BLOCK), lambda i: (0, 0, first + i)),
        out_shape=jax.ShapeDtypeStruct((2, lines, columns), here.dtype),
        input_output_aliases=aliases,
        compiler_params=PARAMS,
        name="azimuth_compress",
    )(*operands)


def passed_back(block, axis):
    size = lax.axis_size(axis)
    return lax.ppermute(block, axis, [(i + 1, i) for i in range(size - 1)])


def edge_routes(az_size, rg_size):
    upper, turn = az_size // 2, rg_size // 2
    flat = lambda i, j: i * rg_size + j
    near, first, second = [], [], []
    for i in range(az_size):
        for j in range(rg_size - 1):
            if j == turn - 1 and i >= az_size - 2:
                first.append((flat(i, turn), flat(i - upper, j)))
                second.append((flat(i - upper, j), flat(i, j)))
            else:
                near.append((flat(i, j + 1), flat(i, j)))
    return near, first, second


def relay_routes(az_size):
    upper = az_size // 2
    ring = upper // 2
    at = lambda z, x, core: z * upper + (x % ring) * 2 + core
    hops = [[], [], []]
    for z in range(2):
        for x in range(ring):
            hops[0].append((at(z, x, 1), at(z, x, 0)))
            if x == 0 and z == 0:
                continue
            to = z if x else z - 1
            hops[0].append((at(z, x, 0), at(to, x + 1, 1)))
            hops[1].append((at(to, x + 1, 1), at(to, x + 2, 1)))
            hops[2].append((at(to, x + 2, 1), at(to, x + 3, 1)))
    return hops


def local(raw, chirp, az_ref, set_index):
    columns = raw.shape[2]
    axes = ("az", "rg")
    near_route, first_route, second_route = edge_routes(lax.axis_size("az"), lax.axis_size("rg"))
    hops = relay_routes(lax.axis_size("az"))
    raw = pltpu.with_memory_space_constraint(raw, pltpu.HBM)
    chirp = pltpu.with_memory_space_constraint(chirp, pltpu.HBM)
    first, edge, near_raw, weights = range_head(raw, chirp, 5)
    turned, second, last_raw = range_fetch(raw, weights, near_raw, first, (1, 3), 2)
    third = range_compress(near_raw, last_raw, weights, second, 2)
    first_next = passed_back(first, "az")
    second_next = passed_back(second, "az")
    third_next = passed_back(third, "az")
    between = lax.ppermute(edge, axes, first_route)
    far = lax.ppermute(between, axes, second_route)
    near = lax.ppermute(edge, axes, near_route)
    carried = [turned]
    for hop in hops:
        carried.append(lax.ppermute(carried[-1], "az", hop))
    fourth = range_tail(last_raw, weights, near, far)
    fourth_next = passed_back(fourth, "az")
    turns = azimuth_weights(set_index, az_ref, third)
    focused = None
    pieces = [
        (first, [first_next], 0),
        (second, [second_next], 2),
        (third, [third_next], 5),
        (turned, [carried[1], carried[3]], 1),
        (fourth, [fourth_next], 7),
    ]
    for here, after, start in pieces:
        focused = azimuth_compress(turns, here, after, focused, columns, start)
    return focused


def solution(mesh):
    in_specs = (P(None, "az", "rg"), P(), P(), P("rg"))
    out_specs = P(None, "az", "rg")
    return jax.shard_map(local, mesh=mesh, in_specs=in_specs, out_specs=out_specs, check_vma=False)
```

```python
import functools

import jax
import jax.numpy as jnp
from jax import lax
from jax.experimental import pallas as pl
from jax.experimental.pallas import tpu as pltpu
from jax.sharding import PartitionSpec as P


LANES = 128
BLOCK = 256
TURNS = 4
VMEM_LIMIT = 16 * 1024 * 1024
WHOLE = pl.BlockSpec(memory_space=pltpu.VMEM)
ANYWHERE = pl.BlockSpec(memory_space=pl.ANY)
PARAMS = pltpu.CompilerParams(vmem_limit_bytes=VMEM_LIMIT)


def shifted_rows(row, count):
    wide = jnp.broadcast_to(row, (count, row.shape[1]))
    return pltpu.roll(wide, 0, 1, stride=1, stride_axis=0)


def build_range_weights(chirp_ref, weights_ref):
    filled = jnp.zeros((2, BLOCK), jnp.float32)
    padded = jnp.concatenate([chirp_ref[...].astype(jnp.float32), filled], axis=1)
    real = jnp.transpose(shifted_rows(padded[0:1], BLOCK)).astype(jnp.bfloat16)
    imag = jnp.transpose(shifted_rows(padded[1:2], BLOCK)).astype(jnp.bfloat16)
    half = 2 * BLOCK
    weights_ref[:half, :BLOCK] = real
    weights_ref[:half, BLOCK:] = -imag
    weights_ref[half:, :BLOCK] = imag
    weights_ref[half:, BLOCK:] = real


def correlate(segment, weights_ref):
    product = jnp.dot(segment, weights_ref[...], preferred_element_type=jnp.float32)
    product = product.astype(jnp.bfloat16)
    return product[:, :BLOCK], product[:, BLOCK:]


def block_at(ref, first, count=1):
    return ref.at[:, :, pl.ds(first * BLOCK, count * BLOCK)]


def head_kernel(
    chirp_hbm, raw_hbm, out_ref, edge_ref, kept_ref, weights_ref, chirp_ref, sems
):
    sources = [chirp_hbm, block_at(raw_hbm, 0)]
    targets = [chirp_ref, edge_ref]
    for k in range(kept_ref.shape[2] // BLOCK):
        sources.append(block_at(raw_hbm, k + 1))
        targets.append(block_at(kept_ref, k))
    copies = [
        pltpu.make_async_copy(source, target, sems.at[k])
        for k, (source, target) in enumerate(zip(sources, targets))
    ]
    for copy in copies:
        copy.start()
    copies[0].wait()
    build_range_weights(chirp_ref, weights_ref)
    copies[1].wait()
    copies[2].wait()
    blocks = [(edge_ref, 0), (kept_ref, 0), (kept_ref, 1)]
    range_blocks((2,), blocks, weights_ref, [out_ref], lambda k: k == 2 and copies[3].wait())
    for copy in copies[4:]:
        copy.wait()


def range_head(raw, chirp, kept):
    lines = raw.shape[1]
    like = lambda *shape: jax.ShapeDtypeStruct(shape, raw.dtype)
    out_shape = [
        like(2, lines, 2 * BLOCK),
        like(2, lines, BLOCK),
        like(2, lines, kept * BLOCK),
        like(4 * BLOCK, 2 * BLOCK),
    ]
    return pl.pallas_call(
        head_kernel,
        in_specs=[ANYWHERE, ANYWHERE],
        out_specs=[WHOLE] * len(out_shape),
        out_shape=out_shape,
        scratch_shapes=[
            pltpu.VMEM(chirp.shape, chirp.dtype),
            pltpu.SemaphoreType.DMA((2 + kept,)),
        ],
        compiler_params=PARAMS,
        name="range_head",
    )(chirp, raw)


def range_blocks(sizes, blocks, weights_ref, outs, arrived=lambda k: None):
    block = 0
    for out_ref, size in zip(outs, sizes):
        for k in range(size):
            arrived(block + 1)
            here_ref, here = blocks[block]
            after_ref, after = blocks[block + 1]
            here = slice(here * BLOCK, (here + 1) * BLOCK)
            after = slice(after * BLOCK, (after + 1) * BLOCK)
            parts = []
            for part in range(2):
                parts += [here_ref[part, :, here], after_ref[part, :, after]]
            real, imag = correlate(jnp.concatenate(parts, axis=1), weights_ref)
            columns = slice(k * BLOCK, (k + 1) * BLOCK)
            out_ref[0, :, columns] = real
            out_ref[1, :, columns] = imag
            block += 1


def fetch_kernel(sizes, weights_ref, near_ref, raw_hbm, previous_ref, *refs):
    outs, kept_ref, sems = refs[: len(sizes)], refs[-2], refs[-1]
    count = kept_ref.shape[2] // BLOCK
    total = raw_hbm.shape[2] // BLOCK
    copies = [
        pltpu.make_async_copy(
            block_at(raw_hbm, total - count + k), block_at(kept_ref, k), sems.at[k]
        )
        for k in range(count)
    ]
    for copy in copies:
        copy.start()
    blocks = [(near_ref, k + 1) for k in range(sum(sizes) + 1)]
    range_blocks(sizes, blocks, weights_ref, outs)
    for copy in copies:
        copy.wait()


def range_fetch(raw, weights, near, previous, sizes, kept):
    lines = raw.shape[1]
    widths = [BLOCK * size for size in sizes] + [BLOCK * kept]
    return pl.pallas_call(
        functools.partial(fetch_kernel, sizes),
        in_specs=[WHOLE, WHOLE, ANYWHERE, ANYWHERE],
        out_specs=[WHOLE] * len(widths),
        out_shape=[jax.ShapeDtypeStruct((2, lines, width), raw.dtype) for width in widths],
        scratch_shapes=[pltpu.SemaphoreType.DMA((kept,))],
        compiler_params=PARAMS,
        name="range_fetch",
    )(weights, near, raw, previous)


def range_kernel(sizes, weights_ref, near_ref, kept_ref, previous_ref, *outs):
    last = near_ref.shape[2] // BLOCK - 1
    blocks = [(near_ref, last)] + [(kept_ref, k) for k in range(sum(sizes))]
    range_blocks(sizes, blocks, weights_ref, outs)


def range_compress(near, kept, weights, previous, sizes):
    lines = near.shape[1]
    return pl.pallas_call(
        functools.partial(range_kernel, sizes),
        in_specs=[WHOLE, WHOLE, WHOLE, ANYWHERE],
        out_specs=[WHOLE] * len(sizes),
        out_shape=[jax.ShapeDtypeStruct((2, lines, BLOCK * size), near.dtype) for size in sizes],
        compiler_params=PARAMS,
        name="range_compress",
    )(weights, near, kept, previous)


def tail_kernel(weights_ref, kept_ref, near_ref, far_ref, out_ref):
    crossing = jnp.logical_and(
        lax.axis_index("rg") == lax.axis_size("rg") // 2 - 1,
        lax.axis_index("az") >= lax.axis_size("az") - 2,
    )
    here = kept_ref[:, :, kept_ref.shape[2] - BLOCK :]
    after = jnp.where(crossing, far_ref[...], near_ref[...])
    segment = jnp.concatenate([here[0], after[0], here[1], after[1]], axis=1)
    out_ref[0], out_ref[1] = correlate(segment, weights_ref)


def range_tail(kept, weights, near, far):
    return pl.pallas_call(
        tail_kernel,
        in_specs=[WHOLE] * 4,
        out_specs=WHOLE,
        out_shape=jax.ShapeDtypeStruct((2, kept.shape[1], BLOCK), kept.dtype),
        compiler_params=PARAMS,
        name="range_tail",
    )(weights, kept, near, far)


def azimuth_weights_kernel(sets_ref, refs_ref, previous_ref, weights_ref, rows_ref):
    filled = jnp.zeros((1, LANES), jnp.float32)

    @pl.when(pl.program_id(0) == 0)
    def _():
        chosen = sets_ref[:, :1]
        shape = (sets_ref.shape[0], refs_ref.shape[1])
        picks = lax.broadcasted_iota(jnp.int32, shape, 1) == chosen
        picks = picks.astype(refs_ref.dtype)
        for part in range(2):
            rows_ref[part] = jnp.dot(picks, refs_ref[part], preferred_element_type=jnp.float32)

    for k in range(TURNS):
        group = pl.program_id(0) * TURNS + k
        for part in range(2):
            row = rows_ref[part, pl.ds(group, 1), :]
            base = shifted_rows(jnp.concatenate([row, filled], axis=1), 16)
            base = base.astype(jnp.bfloat16)
            start = part * LANES
            for q in range(0, LANES, 16):
                both = pltpu.roll(base, q, 1) if q else base
                weights_ref[group, start + q : start + q + 16, :] = both


def azimuth_weights(sets, refs, previous):
    taps = refs.shape[2]
    groups = sets.shape[0] // LANES
    return pl.pallas_call(
        azimuth_weights_kernel,
        grid=(groups // TURNS,),
        in_specs=[WHOLE, WHOLE, ANYWHERE],
        out_specs=WHOLE,
        out_shape=jax.ShapeDtypeStruct((groups, 2 * LANES, taps + LANES), refs.dtype),
        scratch_shapes=[pltpu.VMEM((2, groups, taps), jnp.float32)],
        compiler_params=PARAMS,
        name="azimuth_weights",
    )(sets.reshape(groups, LANES), refs, previous)


def azimuth_kernel(first, relayed, weights_ref, here_ref, after_ref, *rest):
    out_ref = rest[-1]
    by_relay = lax.axis_index("az") % 2 == 1
    lines = here_ref.shape[1]
    span = weights_ref.shape[2] + LANES
    filled = jnp.zeros((LANES, LANES), jnp.bfloat16)
    step = pl.program_id(0)
    for group in range(BLOCK // LANES):
        at = pl.ds(pl.multiple_of(step * BLOCK + group * LANES, LANES), LANES)
        here = jnp.concatenate([here_ref[0, :, at], here_ref[1, :, at]], axis=1)
        after = jnp.concatenate([after_ref[0, :, at], after_ref[1, :, at]], axis=1)
        if relayed:
            other = jnp.concatenate([rest[0][0, :, at], rest[0][1, :, at]], axis=1)
            after = jnp.where(by_relay, other, after)
        whole = jnp.concatenate([here, after], axis=0)
        place = (first + step) * (BLOCK // LANES) + group
        rows = []
        for part in range(2):
            band = weights_ref[place, part * LANES : (part + 1) * LANES]
            rows.append(jnp.concatenate([band, filled], axis=1))
            rows.append(jnp.concatenate([filled, band], axis=1))
        weights = jnp.concatenate(rows, axis=0)
        columns = slice(group * LANES, (group + 1) * LANES)
        for start in range(0, lines, BLOCK):
            product = jnp.dot(
                weights, whole[start : start + span], preferred_element_type=jnp.float32
            )
            real = product[:BLOCK, :LANES] + product[BLOCK:, LANES:]
            imag = product[:BLOCK, LANES:] - product[BLOCK:, :LANES]
            out_ref[0, start : start + BLOCK, columns] = real.astype(out_ref.dtype)
            out_ref[1, start : start + BLOCK, columns] = imag.astype(out_ref.dtype)


def azimuth_compress(weights, here, after, current, columns, first):
    lines = here.shape[1]
    count = here.shape[2] // BLOCK
    operands = [weights, here, *after]
    in_specs = [WHOLE] * len(operands)
    aliases = {}
    if current is not None:
        aliases = {len(operands): 0}
        in_specs.append(ANYWHERE)
        operands.append(current)
    return pl.pallas_call(
        functools.partial(azimuth_kernel, first, len(after) > 1),
        grid=(count,),
        in_specs=in_specs,
        out_specs=pl.BlockSpec((2, lines, BLOCK), lambda i: (0, 0, first + i)),
        out_shape=jax.ShapeDtypeStruct((2, lines, columns), here.dtype),
        input_output_aliases=aliases,
        compiler_params=PARAMS,
        name="azimuth_compress",
    )(*operands)


def passed_back(block, axis):
    size = lax.axis_size(axis)
    return lax.ppermute(block, axis, [(i + 1, i) for i in range(size - 1)])


def edge_routes(az_size, rg_size):
    upper, turn = az_size // 2, rg_size // 2
    flat = lambda i, j: i * rg_size + j
    near, first, second = [], [], []
    for i in range(az_size):
        for j in range(rg_size - 1):
            if j == turn - 1 and i >= az_size - 2:
                between = flat(upper - 2, j if i % 2 else 0)
                first.append((flat(i, turn), between))
                second.append((between, flat(i, j)))
            else:
                near.append((flat(i, j + 1), flat(i, j)))
    return near, first, second


def relay_routes(az_size):
    upper = az_size // 2
    ring = upper // 2
    at = lambda z, x, core: z * upper + (x % ring) * 2 + core
    hops = [[], [], []]
    for z in range(2):
        for x in range(ring):
            hops[0].append((at(z, x, 1), at(z, x, 0)))
            if x == 0 and z == 0:
                continue
            to = z if x else z - 1
            hops[0].append((at(z, x, 0), at(to, x + 1, 1)))
            hops[1].append((at(to, x + 1, 1), at(to, x + 2, 1)))
            hops[2].append((at(to, x + 2, 1), at(to, x + 3, 1)))
    return hops


def local(raw, chirp, az_ref, set_index):
    columns = raw.shape[2]
    axes = ("az", "rg")
    near_route, first_route, second_route = edge_routes(lax.axis_size("az"), lax.axis_size("rg"))
    hops = relay_routes(lax.axis_size("az"))
    raw = pltpu.with_memory_space_constraint(raw, pltpu.HBM)
    chirp = pltpu.with_memory_space_constraint(chirp, pltpu.HBM)
    first, edge, near_raw, weights = range_head(raw, chirp, 3)
    turned, last_raw = range_fetch(raw, weights, near_raw, first, (1,), 4)
    second, third = range_compress(near_raw, last_raw, weights, turned, (2, 2))
    first_next = passed_back(first, "az")
    second_next = passed_back(second, "az")
    third_next = passed_back(third, "az")
    between = lax.ppermute(edge, axes, first_route)
    far = lax.ppermute(between, axes, second_route)
    near = lax.ppermute(edge, axes, near_route)
    carried = [turned]
    for hop in hops:
        carried.append(lax.ppermute(carried[-1], "az", hop))
    fourth = range_tail(last_raw, weights, near, far)
    fourth_next = passed_back(fourth, "az")
    turns = azimuth_weights(set_index, az_ref, third)
    focused = None
    pieces = [
        (first, [first_next], 0),
        (second, [second_next], 3),
        (third, [third_next], 5),
        (turned, [carried[1], carried[3]], 2),
        (fourth, [fourth_next], 7),
    ]
    for k in range(5):
        here, after, start = pieces[k]
        focused = azimuth_compress(turns, here, after, focused, columns, start)
    return focused


def solution(mesh):
    in_specs = (P(None, "az", "rg"), P(), P(), P("rg"))
    out_specs = P(None, "az", "rg")
    return jax.shard_map(local, mesh=mesh, in_specs=in_specs, out_specs=out_specs, check_vma=False)
```

```python
import functools

import jax
import jax.numpy as jnp
from jax import lax
from jax.experimental import pallas as pl
from jax.experimental.pallas import tpu as pltpu
from jax.sharding import PartitionSpec as P


LANES = 128
BLOCK = 256
TURNS = 4
VMEM_LIMIT = 16 * 1024 * 1024
WHOLE = pl.BlockSpec(memory_space=pltpu.VMEM)
ANYWHERE = pl.BlockSpec(memory_space=pl.ANY)
PARAMS = pltpu.CompilerParams(vmem_limit_bytes=VMEM_LIMIT)


def shifted_rows(row, count):
    wide = jnp.broadcast_to(row, (count, row.shape[1]))
    return pltpu.roll(wide, 0, 1, stride=1, stride_axis=0)


def build_range_weights(chirp_ref, weights_ref):
    filled = jnp.zeros((2, BLOCK), jnp.float32)
    padded = jnp.concatenate([chirp_ref[...].astype(jnp.float32), filled], axis=1)
    real = jnp.transpose(shifted_rows(padded[0:1], BLOCK)).astype(jnp.bfloat16)
    imag = jnp.transpose(shifted_rows(padded[1:2], BLOCK)).astype(jnp.bfloat16)
    half = 2 * BLOCK
    weights_ref[:half, :BLOCK] = real
    weights_ref[:half, BLOCK:] = -imag
    weights_ref[half:, :BLOCK] = imag
    weights_ref[half:, BLOCK:] = real


def correlate(segment, weights_ref):
    product = jnp.dot(segment, weights_ref[...], preferred_element_type=jnp.float32)
    product = product.astype(jnp.bfloat16)
    return product[:, :BLOCK], product[:, BLOCK:]


def block_at(ref, first, count=1):
    return ref.at[:, :, pl.ds(first * BLOCK, count * BLOCK)]


def head_kernel(
    chirp_hbm, raw_hbm, out_ref, edge_ref, kept_ref, weights_ref, chirp_ref, sems
):
    sources = [chirp_hbm, block_at(raw_hbm, 0)]
    targets = [chirp_ref, edge_ref]
    for k in range(kept_ref.shape[2] // BLOCK):
        sources.append(block_at(raw_hbm, k + 1))
        targets.append(block_at(kept_ref, k))
    copies = [
        pltpu.make_async_copy(source, target, sems.at[k])
        for k, (source, target) in enumerate(zip(sources, targets))
    ]
    for copy in copies:
        copy.start()
    copies[0].wait()
    build_range_weights(chirp_ref, weights_ref)
    copies[1].wait()
    copies[2].wait()
    blocks = [(edge_ref, 0), (kept_ref, 0), (kept_ref, 1)]
    range_blocks((2,), blocks, weights_ref, [out_ref], lambda k: k == 2 and copies[3].wait())
    for copy in copies[4:]:
        copy.wait()


def range_head(raw, chirp, kept):
    lines = raw.shape[1]
    like = lambda *shape: jax.ShapeDtypeStruct(shape, raw.dtype)
    out_shape = [
        like(2, lines, 2 * BLOCK),
        like(2, lines, BLOCK),
        like(2, lines, kept * BLOCK),
        like(4 * BLOCK, 2 * BLOCK),
    ]
    return pl.pallas_call(
        head_kernel,
        in_specs=[ANYWHERE, ANYWHERE],
        out_specs=[WHOLE] * len(out_shape),
        out_shape=out_shape,
        scratch_shapes=[
            pltpu.VMEM(chirp.shape, chirp.dtype),
            pltpu.SemaphoreType.DMA((2 + kept,)),
        ],
        compiler_params=PARAMS,
        name="range_head",
    )(chirp, raw)


def range_blocks(sizes, blocks, weights_ref, outs, arrived=lambda k: None):
    block = 0
    for out_ref, size in zip(outs, sizes):
        for k in range(size):
            arrived(block + 1)
            here_ref, here = blocks[block]
            after_ref, after = blocks[block + 1]
            here = slice(here * BLOCK, (here + 1) * BLOCK)
            after = slice(after * BLOCK, (after + 1) * BLOCK)
            parts = []
            for part in range(2):
                parts += [here_ref[part, :, here], after_ref[part, :, after]]
            real, imag = correlate(jnp.concatenate(parts, axis=1), weights_ref)
            columns = slice(k * BLOCK, (k + 1) * BLOCK)
            out_ref[0, :, columns] = real
            out_ref[1, :, columns] = imag
            block += 1


def fetch_kernel(sizes, weights_ref, near_ref, raw_hbm, previous_ref, *refs):
    outs, kept_ref, sems = refs[: len(sizes)], refs[-2], refs[-1]
    count = kept_ref.shape[2] // BLOCK
    total = raw_hbm.shape[2] // BLOCK
    copies = [
        pltpu.make_async_copy(
            block_at(raw_hbm, total - count + k), block_at(kept_ref, k), sems.at[k]
        )
        for k in range(count)
    ]
    for copy in copies:
        copy.start()
    blocks = [(near_ref, k + 1) for k in range(sum(sizes) + 1)]
    range_blocks(sizes, blocks, weights_ref, outs)
    for copy in copies:
        copy.wait()


def range_fetch(raw, weights, near, previous, sizes, kept):
    lines = raw.shape[1]
    widths = [BLOCK * size for size in sizes] + [BLOCK * kept]
    return pl.pallas_call(
        functools.partial(fetch_kernel, sizes),
        in_specs=[WHOLE, WHOLE, ANYWHERE, ANYWHERE],
        out_specs=[WHOLE] * len(widths),
        out_shape=[jax.ShapeDtypeStruct((2, lines, width), raw.dtype) for width in widths],
        scratch_shapes=[pltpu.SemaphoreType.DMA((kept,))],
        compiler_params=PARAMS,
        name="range_fetch",
    )(weights, near, raw, previous)


def range_kernel(sizes, weights_ref, near_ref, kept_ref, previous_ref, *outs):
    last = near_ref.shape[2] // BLOCK - 1
    blocks = [(near_ref, last)] + [(kept_ref, k) for k in range(sum(sizes))]
    range_blocks(sizes, blocks, weights_ref, outs)


def range_compress(near, kept, weights, previous, sizes):
    lines = near.shape[1]
    return pl.pallas_call(
        functools.partial(range_kernel, sizes),
        in_specs=[WHOLE, WHOLE, WHOLE, ANYWHERE],
        out_specs=[WHOLE] * len(sizes),
        out_shape=[jax.ShapeDtypeStruct((2, lines, BLOCK * size), near.dtype) for size in sizes],
        compiler_params=PARAMS,
        name="range_compress",
    )(weights, near, kept, previous)


def tail_kernel(weights_ref, kept_ref, near_ref, far_ref, out_ref):
    crossing = jnp.logical_and(
        lax.axis_index("rg") == lax.axis_size("rg") // 2 - 1,
        lax.axis_index("az") >= lax.axis_size("az") - 2,
    )
    here = kept_ref[:, :, kept_ref.shape[2] - BLOCK :]
    after = jnp.where(crossing, far_ref[...], near_ref[...])
    segment = jnp.concatenate([here[0], after[0], here[1], after[1]], axis=1)
    out_ref[0], out_ref[1] = correlate(segment, weights_ref)


def range_tail(kept, weights, near, far):
    return pl.pallas_call(
        tail_kernel,
        in_specs=[WHOLE] * 4,
        out_specs=WHOLE,
        out_shape=jax.ShapeDtypeStruct((2, kept.shape[1], BLOCK), kept.dtype),
        compiler_params=PARAMS,
        name="range_tail",
    )(weights, kept, near, far)


def azimuth_weights_kernel(sets_ref, refs_ref, previous_ref, weights_ref, rows_ref):
    filled = jnp.zeros((1, LANES), jnp.float32)

    @pl.when(pl.program_id(0) == 0)
    def _():
        chosen = sets_ref[:, :1]
        shape = (sets_ref.shape[0], refs_ref.shape[1])
        picks = lax.broadcasted_iota(jnp.int32, shape, 1) == chosen
        picks = picks.astype(refs_ref.dtype)
        for part in range(2):
            rows_ref[part] = jnp.dot(picks, refs_ref[part], preferred_element_type=jnp.float32)

    for k in range(TURNS):
        group = pl.program_id(0) * TURNS + k
        for part in range(2):
            row = rows_ref[part, pl.ds(group, 1), :]
            base = shifted_rows(jnp.concatenate([row, filled], axis=1), 16)
            base = base.astype(jnp.bfloat16)
            start = part * LANES
            for q in range(0, LANES, 16):
                both = pltpu.roll(base, q, 1) if q else base
                weights_ref[group, start + q : start + q + 16, :] = both


def azimuth_weights(sets, refs, previous):
    taps = refs.shape[2]
    groups = sets.shape[0] // LANES
    return pl.pallas_call(
        azimuth_weights_kernel,
        grid=(groups // TURNS,),
        in_specs=[WHOLE, WHOLE, ANYWHERE],
        out_specs=WHOLE,
        out_shape=jax.ShapeDtypeStruct((groups, 2 * LANES, taps + LANES), refs.dtype),
        scratch_shapes=[pltpu.VMEM((2, groups, taps), jnp.float32)],
        compiler_params=PARAMS,
        name="azimuth_weights",
    )(sets.reshape(groups, LANES), refs, previous)


def azimuth_kernel(first, relayed, weights_ref, here_ref, after_ref, *rest):
    out_ref = rest[-1]
    by_relay = lax.axis_index("az") % 2 == 1
    lines = here_ref.shape[1]
    span = weights_ref.shape[2] + LANES
    filled = jnp.zeros((LANES, LANES), jnp.bfloat16)
    step = pl.program_id(0)
    for group in range(BLOCK // LANES):
        at = pl.ds(pl.multiple_of(step * BLOCK + group * LANES, LANES), LANES)
        here = jnp.concatenate([here_ref[0, :, at], here_ref[1, :, at]], axis=1)
        after = jnp.concatenate([after_ref[0, :, at], after_ref[1, :, at]], axis=1)
        if relayed:
            other = jnp.concatenate([rest[0][0, :, at], rest[0][1, :, at]], axis=1)
            after = jnp.where(by_relay, other, after)
        whole = jnp.concatenate([here, after], axis=0)
        place = (first + step) * (BLOCK // LANES) + group
        rows = []
        for part in range(2):
            band = weights_ref[place, part * LANES : (part + 1) * LANES]
            rows.append(jnp.concatenate([band, filled], axis=1))
            rows.append(jnp.concatenate([filled, band], axis=1))
        weights = jnp.concatenate(rows, axis=0)
        columns = slice(group * LANES, (group + 1) * LANES)
        for start in range(0, lines, BLOCK):
            product = jnp.dot(
                weights, whole[start : start + span], preferred_element_type=jnp.float32
            )
            real = product[:BLOCK, :LANES] + product[BLOCK:, LANES:]
            imag = product[:BLOCK, LANES:] - product[BLOCK:, :LANES]
            out_ref[0, start : start + BLOCK, columns] = real.astype(out_ref.dtype)
            out_ref[1, start : start + BLOCK, columns] = imag.astype(out_ref.dtype)


def azimuth_compress(weights, here, after, current, columns, first):
    lines = here.shape[1]
    count = here.shape[2] // BLOCK
    operands = [weights, here, *after]
    in_specs = [WHOLE] * len(operands)
    aliases = {}
    if current is not None:
        aliases = {len(operands): 0}
        in_specs.append(ANYWHERE)
        operands.append(current)
    return pl.pallas_call(
        functools.partial(azimuth_kernel, first, len(after) > 1),
        grid=(count,),
        in_specs=in_specs,
        out_specs=pl.BlockSpec((2, lines, BLOCK), lambda i: (0, 0, first + i)),
        out_shape=jax.ShapeDtypeStruct((2, lines, columns), here.dtype),
        input_output_aliases=aliases,
        compiler_params=PARAMS,
        name="azimuth_compress",
    )(*operands)


def turn_rows(weights_ref, place):
    filled = jnp.zeros((LANES, LANES), jnp.bfloat16)
    rows = []
    for part in range(2):
        band = weights_ref[place, part * LANES : (part + 1) * LANES]
        rows.append(jnp.concatenate([band, filled], axis=1))
        rows.append(jnp.concatenate([filled, band], axis=1))
    return jnp.concatenate(rows, axis=0)


def side_by_side(ref, at):
    return jnp.concatenate([ref[0, :, at], ref[1, :, at]], axis=1)


def combined(product):
    real = product[:BLOCK, :LANES] + product[BLOCK:, LANES:]
    imag = product[:BLOCK, LANES:] - product[BLOCK:, :LANES]
    return real, imag


def own_kernel(first, weights_ref, here_ref, previous_ref, out_ref):
    lines = here_ref.shape[1]
    for group in range(here_ref.shape[2] // LANES):
        at = slice(group * LANES, (group + 1) * LANES)
        weights = turn_rows(weights_ref, first * (BLOCK // LANES) + group)
        here = side_by_side(here_ref, at)
        for start in range(0, lines, BLOCK):
            own = here[start:]
            product = jnp.dot(
                weights[:, : lines - start], own, preferred_element_type=jnp.float32
            )
            real, imag = combined(product)
            out_ref[0, start : start + BLOCK, at] = real
            out_ref[1, start : start + BLOCK, at] = imag


def azimuth_own(weights, here, previous, first):
    return pl.pallas_call(
        functools.partial(own_kernel, first),
        in_specs=[WHOLE, WHOLE, ANYWHERE],
        out_specs=WHOLE,
        out_shape=jax.ShapeDtypeStruct(here.shape, jnp.float32),
        compiler_params=PARAMS,
        name="azimuth_own",
    )(weights, here, previous)


def rest_kernel(first, weights_ref, own_ref, after_ref, current_ref, out_ref):
    lines = after_ref.shape[1]
    group = pl.program_id(0)
    at = pl.ds(pl.multiple_of(group * LANES, LANES), LANES)
    weights = turn_rows(weights_ref, first * (BLOCK // LANES) + group)
    after = side_by_side(after_ref, at)
    span = weights.shape[1]
    for start in range(0, lines, BLOCK):
        reach = start + span - lines
        product = jnp.dot(
            weights[:, span - reach :], after[:reach], preferred_element_type=jnp.float32
        )
        real, imag = combined(product)
        rows = slice(start, start + BLOCK)
        out_ref[0, rows] = (own_ref[0, rows, at] + real).astype(out_ref.dtype)
        out_ref[1, rows] = (own_ref[1, rows, at] + imag).astype(out_ref.dtype)


def azimuth_rest(weights, own, after, current, first):
    lines = after.shape[1]
    groups = after.shape[2] // LANES
    place = first * (BLOCK // LANES)
    return pl.pallas_call(
        functools.partial(rest_kernel, first),
        grid=(groups,),
        in_specs=[WHOLE, WHOLE, WHOLE, ANYWHERE],
        out_specs=pl.BlockSpec((2, lines, LANES), lambda i: (0, 0, place + i)),
        out_shape=jax.ShapeDtypeStruct(current.shape, current.dtype),
        input_output_aliases={3: 0},
        compiler_params=PARAMS,
        name="azimuth_rest",
    )(weights, own, after, current)


def passed_back(block, axis):
    size = lax.axis_size(axis)
    return lax.ppermute(block, axis, [(i + 1, i) for i in range(size - 1)])


def edge_routes(az_size, rg_size):
    upper, turn = az_size // 2, rg_size // 2
    flat = lambda i, j: i * rg_size + j
    near, first, second = [], [], []
    for i in range(az_size):
        for j in range(rg_size - 1):
            if j == turn - 1 and i >= az_size - 2:
                between = flat(upper - 2, j if i % 2 else 0)
                first.append((flat(i, turn), between))
                second.append((between, flat(i, j)))
            else:
                near.append((flat(i, j + 1), flat(i, j)))
    return near, first, second


def relay_routes(az_size):
    upper = az_size // 2
    ring = upper // 2
    at = lambda z, x, core: z * upper + (x % ring) * 2 + core
    hops = [[], [], []]
    for z in range(2):
        for x in range(ring):
            hops[0].append((at(z, x, 1), at(z, x, 0)))
            if x == 0 and z == 0:
                continue
            to = z if x else z - 1
            hops[0].append((at(z, x, 0), at(to, x + 1, 1)))
            hops[1].append((at(to, x + 1, 1), at(to, x + 2, 1)))
            hops[2].append((at(to, x + 2, 1), at(to, x + 3, 1)))
    return hops


def local(raw, chirp, az_ref, set_index):
    columns = raw.shape[2]
    axes = ("az", "rg")
    near_route, first_route, second_route = edge_routes(lax.axis_size("az"), lax.axis_size("rg"))
    hops = relay_routes(lax.axis_size("az"))
    raw = pltpu.with_memory_space_constraint(raw, pltpu.HBM)
    chirp = pltpu.with_memory_space_constraint(chirp, pltpu.HBM)
    first, edge, near_raw, weights = range_head(raw, chirp, 3)
    turned, last_raw = range_fetch(raw, weights, near_raw, first, (1,), 4)
    second, third = range_compress(near_raw, last_raw, weights, turned, (2, 2))
    first_next = passed_back(first, "az")
    second_next = passed_back(second, "az")
    third_next = passed_back(third, "az")
    between = lax.ppermute(edge, axes, first_route)
    far = lax.ppermute(between, axes, second_route)
    near = lax.ppermute(edge, axes, near_route)
    carried = [turned]
    for hop in hops:
        carried.append(lax.ppermute(carried[-1], "az", hop))
    fourth = range_tail(last_raw, weights, near, far)
    fourth_next = passed_back(fourth, "az")
    turns = azimuth_weights(set_index, az_ref, third)
    focused = None
    pieces = [
        (first, [first_next], 0),
        (second, [second_next], 3),
        (third, [third_next], 5),
        (turned, [carried[1], carried[3]], 2),
        (fourth, [fourth_next], 7),
    ]
    for k in range(4):
        here, after, start = pieces[k]
        focused = azimuth_compress(turns, here, after, focused, columns, start)
    here, after, start = pieces[4]
    own = azimuth_own(turns, here, third, start)
    focused = azimuth_rest(turns, own, after[0], focused, start)
    return focused


def solution(mesh):
    in_specs = (P(None, "az", "rg"), P(), P(), P("rg"))
    out_specs = P(None, "az", "rg")
    return jax.shard_map(local, mesh=mesh, in_specs=in_specs, out_specs=out_specs, check_vma=False)
```

```python
import functools

import jax
import jax.numpy as jnp
from jax import lax
from jax.experimental import pallas as pl
from jax.experimental.pallas import tpu as pltpu
from jax.sharding import PartitionSpec as P


LANES = 128
BLOCK = 256
TURNS = 4
VMEM_LIMIT = 16 * 1024 * 1024
WHOLE = pl.BlockSpec(memory_space=pltpu.VMEM)
ANYWHERE = pl.BlockSpec(memory_space=pl.ANY)
PARAMS = pltpu.CompilerParams(vmem_limit_bytes=VMEM_LIMIT)


def shifted_rows(row, count):
    wide = jnp.broadcast_to(row, (count, row.shape[1]))
    return pltpu.roll(wide, 0, 1, stride=1, stride_axis=0)


def build_range_weights(chirp_ref, weights_ref):
    half = 2 * BLOCK
    filled = jnp.zeros((2, BLOCK), jnp.float32)
    padded = jnp.concatenate([chirp_ref[...].astype(jnp.float32), filled], axis=1)
    empty = jnp.zeros((LANES, LANES), jnp.bfloat16)
    tiles = []
    for part in range(2):
        wide = shifted_rows(padded[part : part + 1], LANES)
        near = [
            jnp.transpose(wide[:, d * LANES : (d + 1) * LANES]).astype(jnp.bfloat16)
            for d in range(half // LANES - 1)
        ]
        tiles.append(near)
    real, imag = tiles
    for i in range(half // LANES):
        upper = slice(i * LANES, (i + 1) * LANES)
        lower = slice(half + i * LANES, half + (i + 1) * LANES)
        for j in range(BLOCK // LANES):
            left = slice(j * LANES, (j + 1) * LANES)
            right = slice(BLOCK + j * LANES, BLOCK + (j + 1) * LANES)
            inside = 0 <= i - j < len(real)
            weights_ref[upper, left] = real[i - j] if inside else empty
            weights_ref[lower, right] = real[i - j] if inside else empty
            weights_ref[upper, right] = -imag[i - j] if inside else empty
            weights_ref[lower, left] = imag[i - j] if inside else empty


def correlate(segment, weights_ref):
    product = jnp.dot(segment, weights_ref[...], preferred_element_type=jnp.float32)
    product = product.astype(jnp.bfloat16)
    return product[:, :BLOCK], product[:, BLOCK:]


def block_at(ref, first, count=1):
    return ref.at[:, :, pl.ds(first * BLOCK, count * BLOCK)]


def head_kernel(
    chirp_hbm, raw_hbm, out_ref, edge_ref, kept_ref, weights_ref, chirp_ref, sems
):
    sources = [chirp_hbm, block_at(raw_hbm, 0)]
    targets = [chirp_ref, edge_ref]
    for k in range(kept_ref.shape[2] // BLOCK):
        sources.append(block_at(raw_hbm, k + 1))
        targets.append(block_at(kept_ref, k))
    copies = [
        pltpu.make_async_copy(source, target, sems.at[k])
        for k, (source, target) in enumerate(zip(sources, targets))
    ]
    for copy in copies[:3]:
        copy.start()
    copies[0].wait()
    for copy in copies[3:]:
        copy.start()
    build_range_weights(chirp_ref, weights_ref)
    copies[1].wait()
    copies[2].wait()
    blocks = [(edge_ref, 0), (kept_ref, 0), (kept_ref, 1)]
    range_blocks((2,), blocks, weights_ref, [out_ref], lambda k: k == 2 and copies[3].wait())
    for copy in copies[4:]:
        copy.wait()


def range_head(raw, chirp, kept):
    lines = raw.shape[1]
    like = lambda *shape: jax.ShapeDtypeStruct(shape, raw.dtype)
    out_shape = [
        like(2, lines, 2 * BLOCK),
        like(2, lines, BLOCK),
        like(2, lines, kept * BLOCK),
        like(4 * BLOCK, 2 * BLOCK),
    ]
    return pl.pallas_call(
        head_kernel,
        in_specs=[ANYWHERE, ANYWHERE],
        out_specs=[WHOLE] * len(out_shape),
        out_shape=out_shape,
        scratch_shapes=[
            pltpu.VMEM(chirp.shape, chirp.dtype),
            pltpu.SemaphoreType.DMA((2 + kept,)),
        ],
        compiler_params=PARAMS,
        name="range_head",
    )(chirp, raw)


def range_blocks(sizes, blocks, weights_ref, outs, arrived=lambda k: None):
    block = 0
    for out_ref, size in zip(outs, sizes):
        for k in range(size):
            arrived(block + 1)
            here_ref, here = blocks[block]
            after_ref, after = blocks[block + 1]
            here = slice(here * BLOCK, (here + 1) * BLOCK)
            after = slice(after * BLOCK, (after + 1) * BLOCK)
            parts = []
            for part in range(2):
                parts += [here_ref[part, :, here], after_ref[part, :, after]]
            real, imag = correlate(jnp.concatenate(parts, axis=1), weights_ref)
            columns = slice(k * BLOCK, (k + 1) * BLOCK)
            out_ref[0, :, columns] = real
            out_ref[1, :, columns] = imag
            block += 1


def fetch_kernel(sizes, weights_ref, near_ref, raw_hbm, previous_ref, *refs):
    outs, kept_ref, sems = refs[: len(sizes)], refs[-2], refs[-1]
    count = kept_ref.shape[2] // BLOCK
    total = raw_hbm.shape[2] // BLOCK
    copies = [
        pltpu.make_async_copy(
            block_at(raw_hbm, total - count + k), block_at(kept_ref, k), sems.at[k]
        )
        for k in range(count)
    ]
    for copy in copies:
        copy.start()
    blocks = [(near_ref, k + 1) for k in range(sum(sizes) + 1)]
    range_blocks(sizes, blocks, weights_ref, outs)
    for copy in copies:
        copy.wait()


def range_fetch(raw, weights, near, previous, sizes, kept):
    lines = raw.shape[1]
    widths = [BLOCK * size for size in sizes] + [BLOCK * kept]
    return pl.pallas_call(
        functools.partial(fetch_kernel, sizes),
        in_specs=[WHOLE, WHOLE, ANYWHERE, ANYWHERE],
        out_specs=[WHOLE] * len(widths),
        out_shape=[jax.ShapeDtypeStruct((2, lines, width), raw.dtype) for width in widths],
        scratch_shapes=[pltpu.SemaphoreType.DMA((kept,))],
        compiler_params=PARAMS,
        name="range_fetch",
    )(weights, near, raw, previous)


def range_kernel(sizes, weights_ref, near_ref, kept_ref, previous_ref, *outs):
    last = near_ref.shape[2] // BLOCK - 1
    blocks = [(near_ref, last)] + [(kept_ref, k) for k in range(sum(sizes))]
    range_blocks(sizes, blocks, weights_ref, outs)


def range_compress(near, kept, weights, previous, sizes):
    lines = near.shape[1]
    return pl.pallas_call(
        functools.partial(range_kernel, sizes),
        in_specs=[WHOLE, WHOLE, WHOLE, ANYWHERE],
        out_specs=[WHOLE] * len(sizes),
        out_shape=[jax.ShapeDtypeStruct((2, lines, BLOCK * size), near.dtype) for size in sizes],
        compiler_params=PARAMS,
        name="range_compress",
    )(weights, near, kept, previous)


def tail_kernel(weights_ref, kept_ref, near_ref, far_ref, out_ref):
    crossing = jnp.logical_and(
        lax.axis_index("rg") == lax.axis_size("rg") // 2 - 1,
        lax.axis_index("az") >= lax.axis_size("az") - 2,
    )
    here = kept_ref[:, :, kept_ref.shape[2] - BLOCK :]
    after = jnp.where(crossing, far_ref[...], near_ref[...])
    segment = jnp.concatenate([here[0], after[0], here[1], after[1]], axis=1)
    out_ref[0], out_ref[1] = correlate(segment, weights_ref)


def range_tail(kept, weights, near, far):
    return pl.pallas_call(
        tail_kernel,
        in_specs=[WHOLE] * 4,
        out_specs=WHOLE,
        out_shape=jax.ShapeDtypeStruct((2, kept.shape[1], BLOCK), kept.dtype),
        compiler_params=PARAMS,
        name="range_tail",
    )(weights, kept, near, far)


def azimuth_weights_kernel(sets_ref, refs_ref, previous_ref, weights_ref, rows_ref):
    filled = jnp.zeros((1, LANES), jnp.float32)

    @pl.when(pl.program_id(0) == 0)
    def _():
        chosen = sets_ref[:, :1]
        shape = (sets_ref.shape[0], refs_ref.shape[1])
        picks = lax.broadcasted_iota(jnp.int32, shape, 1) == chosen
        picks = picks.astype(refs_ref.dtype)
        for part in range(2):
            rows_ref[part] = jnp.dot(picks, refs_ref[part], preferred_element_type=jnp.float32)

    for k in range(TURNS):
        group = pl.program_id(0) * TURNS + k
        for part in range(2):
            row = rows_ref[part, pl.ds(group, 1), :]
            base = shifted_rows(jnp.concatenate([row, filled], axis=1), 16)
            base = base.astype(jnp.bfloat16)
            start = part * LANES
            for q in range(0, LANES, 16):
                both = pltpu.roll(base, q, 1) if q else base
                weights_ref[group, start + q : start + q + 16, :] = both


def azimuth_weights(sets, refs, previous):
    taps = refs.shape[2]
    groups = sets.shape[0] // LANES
    return pl.pallas_call(
        azimuth_weights_kernel,
        grid=(groups // TURNS,),
        in_specs=[WHOLE, WHOLE, ANYWHERE],
        out_specs=WHOLE,
        out_shape=jax.ShapeDtypeStruct((groups, 2 * LANES, taps + LANES), refs.dtype),
        scratch_shapes=[pltpu.VMEM((2, groups, taps), jnp.float32)],
        compiler_params=PARAMS,
        name="azimuth_weights",
    )(sets.reshape(groups, LANES), refs, previous)


def azimuth_kernel(first, relayed, weights_ref, here_ref, after_ref, *rest):
    out_ref = rest[-1]
    by_relay = lax.axis_index("az") % 2 == 1
    lines = here_ref.shape[1]
    span = weights_ref.shape[2] + LANES
    filled = jnp.zeros((LANES, LANES), jnp.bfloat16)
    step = pl.program_id(0)
    for group in range(BLOCK // LANES):
        at = pl.ds(pl.multiple_of(step * BLOCK + group * LANES, LANES), LANES)
        here = jnp.concatenate([here_ref[0, :, at], here_ref[1, :, at]], axis=1)
        after = jnp.concatenate([after_ref[0, :, at], after_ref[1, :, at]], axis=1)
        if relayed:
            other = jnp.concatenate([rest[0][0, :, at], rest[0][1, :, at]], axis=1)
            after = jnp.where(by_relay, other, after)
        whole = jnp.concatenate([here, after], axis=0)
        place = (first + step) * (BLOCK // LANES) + group
        rows = []
        for part in range(2):
            band = weights_ref[place, part * LANES : (part + 1) * LANES]
            rows.append(jnp.concatenate([band, filled], axis=1))
            rows.append(jnp.concatenate([filled, band], axis=1))
        weights = jnp.concatenate(rows, axis=0)
        columns = slice(group * LANES, (group + 1) * LANES)
        for start in range(0, lines, BLOCK):
            product = jnp.dot(
                weights, whole[start : start + span], preferred_element_type=jnp.float32
            )
            real = product[:BLOCK, :LANES] + product[BLOCK:, LANES:]
            imag = product[:BLOCK, LANES:] - product[BLOCK:, :LANES]
            out_ref[0, start : start + BLOCK, columns] = real.astype(out_ref.dtype)
            out_ref[1, start : start + BLOCK, columns] = imag.astype(out_ref.dtype)


def azimuth_compress(weights, here, after, current, columns, first):
    lines = here.shape[1]
    count = here.shape[2] // BLOCK
    operands = [weights, here, *after]
    in_specs = [WHOLE] * len(operands)
    aliases = {}
    if current is not None:
        aliases = {len(operands): 0}
        in_specs.append(ANYWHERE)
        operands.append(current)
    return pl.pallas_call(
        functools.partial(azimuth_kernel, first, len(after) > 1),
        grid=(count,),
        in_specs=in_specs,
        out_specs=pl.BlockSpec((2, lines, BLOCK), lambda i: (0, 0, first + i)),
        out_shape=jax.ShapeDtypeStruct((2, lines, columns), here.dtype),
        input_output_aliases=aliases,
        compiler_params=PARAMS,
        name="azimuth_compress",
    )(*operands)


def turn_rows(weights_ref, place):
    filled = jnp.zeros((LANES, LANES), jnp.bfloat16)
    rows = []
    for part in range(2):
        band = weights_ref[place, part * LANES : (part + 1) * LANES]
        rows.append(jnp.concatenate([band, filled], axis=1))
        rows.append(jnp.concatenate([filled, band], axis=1))
    return jnp.concatenate(rows, axis=0)


def side_by_side(ref, at):
    return jnp.concatenate([ref[0, :, at], ref[1, :, at]], axis=1)


def combined(product):
    real = product[:BLOCK, :LANES] + product[BLOCK:, LANES:]
    imag = product[:BLOCK, LANES:] - product[BLOCK:, :LANES]
    return real, imag


def own_kernel(first, weights_ref, here_ref, previous_ref, out_ref):
    lines = here_ref.shape[1]
    for group in range(here_ref.shape[2] // LANES):
        at = slice(group * LANES, (group + 1) * LANES)
        weights = turn_rows(weights_ref, first * (BLOCK // LANES) + group)
        here = side_by_side(here_ref, at)
        for start in range(0, lines, BLOCK):
            own = here[start:]
            product = jnp.dot(
                weights[:, : lines - start], own, preferred_element_type=jnp.float32
            )
            real, imag = combined(product)
            out_ref[0, start : start + BLOCK, at] = real
            out_ref[1, start : start + BLOCK, at] = imag


def azimuth_own(weights, here, previous, first):
    return pl.pallas_call(
        functools.partial(own_kernel, first),
        in_specs=[WHOLE, WHOLE, ANYWHERE],
        out_specs=WHOLE,
        out_shape=jax.ShapeDtypeStruct(here.shape, jnp.float32),
        compiler_params=PARAMS,
        name="azimuth_own",
    )(weights, here, previous)


def rest_kernel(first, weights_ref, own_ref, after_ref, current_ref, out_ref):
    lines = after_ref.shape[1]
    for group in range(after_ref.shape[2] // LANES):
        at = slice(group * LANES, (group + 1) * LANES)
        weights = turn_rows(weights_ref, first * (BLOCK // LANES) + group)
        after = side_by_side(after_ref, at)
        span = weights.shape[1]
        for start in range(0, lines, BLOCK):
            reach = start + span - lines
            product = jnp.dot(
                weights[:, span - reach :], after[:reach], preferred_element_type=jnp.float32
            )
            real, imag = combined(product)
            rows = slice(start, start + BLOCK)
            out_ref[0, rows, at] = (own_ref[0, rows, at] + real).astype(out_ref.dtype)
            out_ref[1, rows, at] = (own_ref[1, rows, at] + imag).astype(out_ref.dtype)


def azimuth_rest(weights, own, after, current, first):
    return pl.pallas_call(
        functools.partial(rest_kernel, first),
        grid=(1,),
        in_specs=[WHOLE, WHOLE, WHOLE, ANYWHERE],
        out_specs=pl.BlockSpec(after.shape, lambda i: (0, 0, first)),
        out_shape=jax.ShapeDtypeStruct(current.shape, current.dtype),
        input_output_aliases={3: 0},
        compiler_params=PARAMS,
        name="azimuth_rest",
    )(weights, own, after, current)


def passed_back(block, axis):
    size = lax.axis_size(axis)
    return lax.ppermute(block, axis, [(i + 1, i) for i in range(size - 1)])


def edge_routes(az_size, rg_size):
    upper, turn = az_size // 2, rg_size // 2
    flat = lambda i, j: i * rg_size + j
    near, first, second = [], [], []
    for i in range(az_size):
        for j in range(rg_size - 1):
            if j == turn - 1 and i >= az_size - 2:
                between = flat(upper - 2, j if i % 2 else 0)
                first.append((flat(i, turn), between))
                second.append((between, flat(i, j)))
            else:
                near.append((flat(i, j + 1), flat(i, j)))
    return near, first, second


def relay_routes(az_size):
    upper = az_size // 2
    ring = upper // 2
    at = lambda z, x, core: z * upper + (x % ring) * 2 + core
    hops = [[], [], []]
    for z in range(2):
        for x in range(ring):
            hops[0].append((at(z, x, 1), at(z, x, 0)))
            if x == 0 and z == 0:
                continue
            to = z if x else z - 1
            hops[0].append((at(z, x, 0), at(to, x + 1, 1)))
            hops[1].append((at(to, x + 1, 1), at(to, x + 2, 1)))
            hops[2].append((at(to, x + 2, 1), at(to, x + 3, 1)))
    return hops


def local(raw, chirp, az_ref, set_index):
    columns = raw.shape[2]
    axes = ("az", "rg")
    near_route, first_route, second_route = edge_routes(lax.axis_size("az"), lax.axis_size("rg"))
    hops = relay_routes(lax.axis_size("az"))
    raw = pltpu.with_memory_space_constraint(raw, pltpu.HBM)
    chirp = pltpu.with_memory_space_constraint(chirp, pltpu.HBM)
    first, edge, near_raw, weights = range_head(raw, chirp, 3)
    turned, last_raw = range_fetch(raw, weights, near_raw, first, (1,), 4)
    second, third = range_compress(near_raw, last_raw, weights, turned, (2, 2))
    first_next = passed_back(first, "az")
    second_next = passed_back(second, "az")
    third_next = passed_back(third, "az")
    between = lax.ppermute(edge, axes, first_route)
    far = lax.ppermute(between, axes, second_route)
    near = lax.ppermute(edge, axes, near_route)
    carried = [turned]
    for hop in hops:
        carried.append(lax.ppermute(carried[-1], "az", hop))
    fourth = range_tail(last_raw, weights, near, far)
    fourth_next = passed_back(fourth, "az")
    turns = azimuth_weights(set_index, az_ref, third)
    focused = None
    pieces = [
        (first, [first_next], 0),
        (second, [second_next], 3),
        (third, [third_next], 5),
        (turned, [carried[1], carried[3]], 2),
        (fourth, [fourth_next], 7),
    ]
    for k in range(4):
        here, after, start = pieces[k]
        focused = azimuth_compress(turns, here, after, focused, columns, start)
    here, after, start = pieces[4]
    own = azimuth_own(turns, here, third, start)
    focused = azimuth_rest(turns, own, after[0], focused, start)
    return focused


def solution(mesh):
    in_specs = (P(None, "az", "rg"), P(), P(), P("rg"))
    out_specs = P(None, "az", "rg")
    return jax.shard_map(local, mesh=mesh, in_specs=in_specs, out_specs=out_specs, check_vma=False)
```
